256 devices in a mesh: tm: 8 (over x_lo, y), space: 32 (over x_hi, z, core).
Axes of the slice: x: 4 (x_hi: 2, x_lo: 2; x = x_hi * 2 + x_lo), y: 4, z: 8, core: 2. Of those that a mesh axis runs over, the one named last changes fastest.
Arguments:
- source: float32 [32, 128, 96, 128], P('tm', 'space'), may hold values from -6 to 6
- initial: float32 [128, 96, 128], P('space'), may hold values from -6 to 6
- mobility: float32 [128, 96, 128], P('space'), may hold values from 0.5 to 2
- labels: int32 [128, 96, 128], P('space'), may hold values from 0 to 3
- electrode: int32 [128, 96, 128], P('space'), may hold values 0 or 1
- rates: float32 [4], replicated, may hold values from 0.2 to 1
Outputs:
- density: float32 [32, 128, 96, 128], P('tm', 'space')
The draws below stay inside these ranges and needn't reach their ends.
All inputs are finite; a program needn't handle non-finite values. No bound on the sum of `electrode` on one device may be relied on, other than what follows from the above.
Results may differ from the reference program's by a relative error of at most 0.00002.
Values sent between devices are 32-bit elements; how exact they have to be, the bound alone decides.
No kernel may reach another device: no remote copies, remote signals or barrier semaphores. Data moves between devices by JAX's collectives and lax.ppermute only.
A program may use at most 64 MiB of HBM per device.

```python
import math
import jax
import jax.numpy as jnp
from jax import lax

TS = 4
NY = 96
NZ = 128
PASSES = 4
PRE = 1
POST = 1
REGIONS = 4
NT = 32
NX = 128
N_TM = 8


def touch_ends(array, rng, least, high):
    longest = array.shape.index(max(array.shape))
    spots = []
    for shift in (0, 1):
        where = [jax.random.randint(jax.random.fold_in(rng, axis), (), 0, length) for axis, length in enumerate(array.shape)]
        where[longest] = (where[longest] + shift) % array.shape[longest]
        spots.append(tuple(where))
    return array.at[spots[0]].set(least).at[spots[1]].set(high)


def shard_levels(rng, dims, cuts, smallest, largest):
    def one(dim, parts):
        draws = jax.random.uniform(jax.random.fold_in(jax.random.fold_in(rng, 6), dim), (parts,), jnp.float32, smallest / len(cuts), largest / len(cuts))
        return jnp.repeat(jnp.exp(draws), dims[dim] // parts).reshape((-1,) + (1,) * (len(dims) - dim - 1))

    factor_of = one(*cuts[0])
    for cut in cuts[1:]:
        factor_of = factor_of * one(*cut)
    return factor_of


def normal_values(own_key, dims, width, reach, cuts=(), kind=jnp.bfloat16):
    result = jax.random.normal(own_key, dims, jnp.float32) * width
    if len(cuts) > 0:
        result = shard_levels(own_key, dims, cuts, -0.22, 0.18) * result
    return jnp.clip(result, min=-reach, max=reach).astype(kind)


def setup_inputs(seed: int = 0) -> dict:
    key_list = jax.random.split(jax.random.key(seed), 7)
    return {
        "source": normal_values(key_list[0], (NT, NX, NY, NZ), 1.0, 6.0, ((0, 8), (1, 32)), jnp.float32),
        "initial": normal_values(key_list[1], (NX, NY, NZ), 1.0, 6.0, ((0, 32),), jnp.float32),
        "mobility": jnp.clip(jnp.exp(math.log(2.0) - 1.3862944 * jax.random.uniform(key_list[2], (NX, NY, NZ), jnp.float32) ** shard_levels(key_list[2], (NX, NY, NZ), ((0, 32),), -0.2, 0.2)), 0.5, 2.0),
        "labels": touch_ends(jax.random.randint(key_list[3], (NX, NY, NZ), 0, REGIONS), jax.random.fold_in(key_list[3], 1), 0, REGIONS - 1).astype(jnp.int32),
        "electrode": touch_ends((jax.random.randint(key_list[4], (NX, NY, NZ), 0, 8) < 1).astype(jnp.int32), jax.random.fold_in(key_list[4], 1), 0, 1),
        "rates": jnp.clip(jnp.exp(jax.random.uniform(key_list[5], (REGIONS,), jnp.float32, math.log(0.2), math.log(1.0))), 0.2, 1.0),
    }


source_coef = 0.5
drift_coef = 0.5
react_coef = 0.5
damping = 0.8
coarse_lateral = 0.06
coarse_axial = 0.12


def pad_across(values):
    return jnp.pad(values, ((0, 0), (0, 0), (1, 1), (1, 1)))


def balance(window, mobile, rate_field, forcing):
    current = window[1:, 1:-1]
    former = window[:-1, 1:-1]
    middle = mobile[:, 1:-1]
    spread = pad_across(middle)
    below_x = 0.5 * (middle + mobile[:, :-2])
    above_x = 0.5 * (middle + mobile[:, 2:])
    below_y = 0.5 * (middle + spread[:, :, :-2, 1:-1])
    above_y = 0.5 * (middle + spread[:, :, 2:, 1:-1])
    below_z = 0.5 * (middle + spread[:, :, 1:-1, :-2])
    above_z = 0.5 * (middle + spread[:, :, 1:-1, 2:])
    beside_all = pad_across(current)
    lower_z = beside_all[:, :, 1:-1, :-2]
    summed = below_x + above_x + below_y + above_y + below_z + above_z
    inflow = (below_x * window[1:, :-2] + above_x * window[1:, 2:]
              + below_y * beside_all[:, :, :-2, 1:-1] + above_y * beside_all[:, :, 2:, 1:-1]
              + below_z * lower_z + above_z * beside_all[:, :, 1:-1, 2:] - summed * current)
    carried = below_z * lower_z - above_z * current
    magnitude = jnp.abs(current)
    excess = current - former - inflow - drift_coef * carried + react_coef * rate_field * current * magnitude
    residue = forcing - excess
    diagonal = 1.0 + summed + drift_coef * above_z + rate_field * magnitude
    return residue, diagonal, current


def relax(window, mobile, rate_field, freedom, forcing):
    residue, diagonal, current = balance(window, mobile, rate_field, forcing)
    updated = current + damping * freedom * residue / diagonal
    return jnp.concatenate([window[:1, 1:-1], updated], axis=0)


def coarse_change(extended, mobility_ext):
    centre = extended[1:-1, 1:-1]
    centre_mob = mobility_ext[1:-1, 1:-1]
    padded_value = jnp.pad(centre, ((0, 0), (0, 0), (1, 1)))
    padded_mob = jnp.pad(centre_mob, ((0, 0), (0, 0), (1, 1)))

    def couple(value_near, mobile_near):
        return 0.5 * (centre_mob + mobile_near) * (value_near - centre)

    lateral = (couple(extended[:-2, 1:-1], mobility_ext[:-2, 1:-1])
               + couple(extended[2:, 1:-1], mobility_ext[2:, 1:-1])
               + couple(extended[1:-1, :-2], mobility_ext[1:-1, :-2])
               + couple(extended[1:-1, 2:], mobility_ext[1:-1, 2:]))
    along_z = couple(padded_value[:, :, :-2], padded_mob[:, :, :-2]) + couple(padded_value[:, :, 2:], padded_mob[:, :, 2:])
    return centre + coarse_lateral * lateral + coarse_axial * along_z


def region_rates(labels, rates):
    matches = labels[None] == jnp.arange(rates.shape[0], dtype=jnp.int32)[:, None, None, None]
    return jnp.sum(jnp.where(matches, rates[:, None, None, None], 0.0), axis=0)


def restrict(residue):
    step_count, planes, across, depth_z = residue.shape
    grouped = residue.reshape(step_count // 4, 4, planes // 2, 2, across // 2, 2, depth_z)
    return 0.25 * jnp.sum(grouped, axis=(1, 3, 5))


def coarse_mobility(mobility):
    planes, across, depth_z = mobility.shape
    return 0.25 * jnp.sum(mobility.reshape(planes // 2, 2, across // 2, 2, depth_z), axis=(1, 3))


def prolong(correction):
    return jnp.repeat(jnp.repeat(jnp.repeat(correction, 4, axis=0), 2, axis=1), 2, axis=2)


def reference(source, initial, mobility, labels, electrode, rates):
    rate_field = region_rates(labels, rates)[None]
    freedom = (1.0 - electrode.astype(jnp.float32))[None]
    forcing = source_coef * source
    padded_mob = jnp.pad(mobility, ((1, 1), (0, 0), (0, 0)))[None]
    layout = (N_TM, TS) + initial.shape
    forcing_blocks = forcing.reshape(layout)

    def pad_planes(window):
        return jnp.pad(window, ((0, 0), (1, 1), (0, 0), (0, 0)))

    def windows(iterate):
        blocks = iterate.reshape(layout)
        before = jnp.concatenate([initial[None], blocks[:-1, -1]], axis=0)
        return blocks, before

    def sweep(iterate):
        blocks, before = windows(iterate)

        def per_block(members):
            time_block, opening, pushed = members
            window = jnp.concatenate([opening[None], time_block], axis=0)
            for number in range(PASSES):
                window = relax(pad_planes(window), padded_mob, rate_field, freedom, pushed)
            return window[1:]

        return lax.map(per_block, (blocks, before, forcing_blocks)).reshape(iterate.shape)

    def residual_of(iterate):
        blocks, before = windows(iterate)

        def per_block(members):
            time_block, opening, pushed = members
            window = jnp.concatenate([opening[None], time_block], axis=0)
            return balance(pad_planes(window), padded_mob, rate_field, pushed)[0]

        return lax.map(per_block, (blocks, before, forcing_blocks)).reshape(iterate.shape)

    iterate = jnp.broadcast_to(initial, source.shape)
    for number in range(PRE):
        iterate = sweep(iterate)
    coarse_rhs = restrict(residual_of(iterate))
    mob_ext = jnp.pad(coarse_mobility(mobility), ((1, 1), (1, 1), (0, 0)))

    def advance(carry_state, forcing_row):
        advanced = coarse_change(jnp.pad(carry_state, ((1, 1), (1, 1), (0, 0))), mob_ext) + forcing_row
        return advanced, advanced

    final_state, history = lax.scan(advance, jnp.zeros(coarse_rhs.shape[1:], jnp.float32), coarse_rhs)
    iterate = iterate + freedom * prolong(history)
    for number in range(POST):
        iterate = sweep(iterate)
    return iterate
```

```python
import jax
import jax.numpy as jnp
from jax import lax
from jax.sharding import PartitionSpec as P

PASSES = 4
DAMPING = 0.8
LATERAL = 0.06
AXIAL = 0.12


def pad_across(values):
    return jnp.pad(values, ((0, 0), (0, 0), (1, 1), (1, 1)))


def balance(cells, former, mobile, rate_field, forcing):
    current = cells[:, 1:-1]
    middle = mobile[:, 1:-1]
    spread = pad_across(middle)
    below_x = 0.5 * (middle + mobile[:, :-2])
    above_x = 0.5 * (middle + mobile[:, 2:])
    below_y = 0.5 * (middle + spread[:, :, :-2, 1:-1])
    above_y = 0.5 * (middle + spread[:, :, 2:, 1:-1])
    below_z = 0.5 * (middle + spread[:, :, 1:-1, :-2])
    above_z = 0.5 * (middle + spread[:, :, 1:-1, 2:])
    beside_all = pad_across(current)
    lower_z = beside_all[:, :, 1:-1, :-2]
    summed = below_x + above_x + below_y + above_y + below_z + above_z
    inflow = (
        below_x * cells[:, :-2]
        + above_x * cells[:, 2:]
        + below_y * beside_all[:, :, :-2, 1:-1]
        + above_y * beside_all[:, :, 2:, 1:-1]
        + below_z * lower_z
        + above_z * beside_all[:, :, 1:-1, 2:]
        - summed * current
    )
    carried = below_z * lower_z - above_z * current
    magnitude = jnp.abs(current)
    excess = current - former - inflow - 0.5 * carried + 0.5 * rate_field * current * magnitude
    residue = forcing - excess
    diagonal = 1.0 + summed + 0.5 * above_z + rate_field * magnitude
    return (residue, diagonal, current)


def inner(values, dim, cut):
    return lax.slice_in_dim(values, cut, values.shape[dim] - cut, axis=dim)


def sweep(cells, opening, mobile, rate_field, freedom, forcing):
    for number in range(PASSES):
        first = inner(opening, 0, number)[None]
        former = jnp.concatenate([first, cells[:-1, 1:-1]], axis=0)
        residue, diagonal, current = balance(
            cells,
            former,
            inner(mobile, 0, number)[None],
            inner(rate_field, 0, number)[None],
            inner(forcing, 1, number),
        )
        cells = current + DAMPING * inner(freedom, 0, number)[None] * residue / diagonal
    return cells


def region_rates(labels, rates):
    matches = labels[None] == jnp.arange(rates.shape[0], dtype=jnp.int32)[:, None, None, None]
    return jnp.sum(jnp.where(matches, rates[:, None, None, None], 0.0), axis=0)


def coarsen(values):
    lead = values.shape[:-3]
    planes, across, depth_z = values.shape[-3:]
    grouped = values.reshape(lead + (planes // 2, 2, across // 2, 2, depth_z))
    return 0.25 * jnp.sum(grouped, axis=(-4, -2))


def prolong(correction):
    return jnp.repeat(jnp.repeat(correction, 2, axis=-3), 2, axis=-2)


class Coupling:
    def __init__(self, mob, inside):
        centre = mob[1:-1]
        padded = jnp.pad(centre, ((0, 0), (1, 1), (1, 1)))
        keep = inside[1:-1, None, None]
        half = 0.5 * LATERAL * keep
        axial = 0.5 * AXIAL * keep
        self.xl = half * (centre + mob[:-2])
        self.xh = half * (centre + mob[2:])
        self.yl = half * (centre + padded[:, :-2, 1:-1])
        self.yh = half * (centre + padded[:, 2:, 1:-1])
        self.zl = axial * (centre + padded[:, 1:-1, :-2])
        self.zh = axial * (centre + padded[:, 1:-1, 2:])
        self.own = keep - (self.xl + self.xh + self.yl + self.yh + self.zl + self.zh)

    def step(self, values):
        planes = values.shape[-3] - 2
        cut = (self.own.shape[0] - planes) // 2
        take = lambda w: inner(w, 0, cut)
        centre = values[..., 1:-1, :, :]
        pads = [(0, 0)] * (values.ndim - 2) + [(1, 1), (1, 1)]
        padded = jnp.pad(centre, pads)
        return (
            take(self.own) * centre
            + take(self.xl) * values[..., :-2, :, :]
            + take(self.xh) * values[..., 2:, :, :]
            + take(self.yl) * padded[..., :-2, 1:-1]
            + take(self.yh) * padded[..., 2:, 1:-1]
            + take(self.zl) * padded[..., 1:-1, :-2]
            + take(self.zh) * padded[..., 1:-1, 2:]
        )

    def steps(self, values, count):
        for number in range(count):
            values = self.step(values)
        return values


def swap(low, high):
    count = lax.axis_size("space")
    odd = lax.axis_index("space") % 2 == 1
    far_pairs = [(i, i + 1 if i % 2 else i - 1) for i in range(1, count - 1)]
    near_pairs = [(i, i ^ 1) for i in range(count)]
    far = lax.ppermute(jnp.where(odd, high, low), "space", far_pairs)
    near = lax.ppermute(jnp.where(odd, low, high), "space", near_pairs)
    return jnp.where(odd, near, far), jnp.where(odd, far, near)


def arrived(value, steps, shift=0):
    times = lax.axis_size("tm")
    count = lax.axis_size("space")
    if shift == 0:
        return lax.ppermute(value, "tm", [(k, k + steps) for k in range(times - steps)])
    pairs = [
        (k * count + s + shift, (k + steps) * count + s)
        for k in range(times - steps)
        for s in range(count)
        if 0 <= s + shift < count
    ]
    return lax.ppermute(value, ("tm", "space"), pairs)


def on_device(source, initial, mobility, labels, electrode, rates):
    slab = initial.shape[0]
    place = lax.axis_index("space")
    leading = lax.axis_index("tm") == 0
    rate_field = region_rates(labels, rates)
    freedom = 1.0 - electrode.astype(jnp.float32)
    forcing = 0.5 * source
    inside = lambda reach: (
        (2 * place + jnp.arange(-reach, 2 + reach) >= 0)
        & (2 * place + jnp.arange(-reach, 2 + reach) < 2 * lax.axis_size("space"))
    ).astype(jnp.float32)
    flat = lambda v: v.reshape((-1,) + v.shape[-2:])

    def parcel(begin):
        part = slice(begin, begin + slab - 1)
        return jnp.concatenate(
            [flat(forcing[:, part]), initial, mobility, freedom, rate_field[part]], axis=0
        )

    def unpack(block):
        count = slab - 1
        sizes = [4 * count, slab, slab, slab, count]
        out = []
        at = 0
        for size in sizes:
            out.append(block[at : at + size])
            at += size
        out[0] = out[0].reshape((4, count) + block.shape[-2:])
        return out

    below, above = swap(parcel(0), parcel(1))
    below, above = unpack(below), unpack(above)
    wide = lambda i, own, dim=0: jnp.concatenate([below[i], own, above[i]], axis=dim)
    forcing_w = wide(0, forcing, 1)
    initial_w = wide(1, initial)
    mobility_w = wide(2, mobility)
    freedom_w = wide(3, freedom)
    rate_w = wide(4, rate_field)

    start = jnp.broadcast_to(initial_w, (4,) + initial_w.shape)
    first = sweep(start, inner(initial_w, 0, 1), mobility_w, rate_w, inner(freedom_w, 0, 1), forcing_w)

    rough = coarsen(mobility_w)
    block = flat(first)
    pack = lambda c: c.reshape((-1,) + block.shape[-2:])
    low, high = swap(
        jnp.concatenate([block, pack(rough[4:6])], axis=0),
        jnp.concatenate([block, pack(rough[0:2])], axis=0),
    )
    side = lambda b: b[: 4 * slab].reshape((4, slab) + b.shape[-2:])
    coarse_shape = rough.shape[1:]
    rough_of = lambda b: b[4 * slab :].reshape((2,) + coarse_shape)
    states = jnp.concatenate([side(low), first, side(high)], axis=1)
    rough_w = jnp.concatenate([rough_of(low), rough, rough_of(high)], axis=0)

    near = inner(states, 1, 1)
    opening0 = jnp.where(leading, inner(initial_w, 0, 2), 0.0)
    former = jnp.concatenate([opening0[None], inner(states, 1, 2)[:-1]], axis=0)
    residue = balance(
        near,
        former,
        inner(mobility_w, 0, 1)[None],
        inner(rate_w, 0, 1)[None],
        inner(forcing_w, 1, 1),
    )[0]
    base = coarsen(jnp.sum(residue, axis=0)) * inside(1)[:, None, None]
    closing = coarsen(inner(states[3], 0, 2))

    both = jnp.stack([base, closing])
    one = arrived(both, 1)
    two = arrived(both, 2)
    three = arrived(closing, 3)
    opening = arrived(inner(states[3], 0, 1), 1)

    coupling1 = Coupling(inner(rough_w, 0, 2), inside(2))
    rhs = base + one[1]
    rhs1 = one[0] + two[1]
    rhs2 = two[0] + three
    pair = jnp.stack([inner(rhs, 0, 1), inner(rhs1, 0, 1)])
    pair = pair + Coupling(inner(rough_w, 0, 3), inside(1)).step(jnp.stack([rhs1, rhs2]))

    older = [arrived(pair, 2, d) for d in (-1, 0, 1)]
    older = jnp.concatenate(older, axis=1)
    pair = pair + coupling1.steps(older, 2)

    cargo = lambda c: jnp.concatenate([pair.reshape((4,) + coarse_shape), c], axis=0)
    low, high = swap(cargo(rough_w[8:10]), cargo(rough_w[0:2]))
    older = [arrived(pair, 4, d) for d in (-3, -2, -1, 0, 1, 2, 3)]
    older = jnp.concatenate(older, axis=1)
    pair_of = lambda b: b[:4].reshape(pair.shape)
    rough_far = jnp.concatenate([low[4:], rough_w, high[4:]], axis=0)
    pair_w = jnp.concatenate([pair_of(low), pair, pair_of(high)], axis=1)
    correction = pair_w + Coupling(rough_far, inside(6)).steps(older, 4)

    fine = prolong(correction)
    cells = states + freedom_w[None] * fine[0][None]
    near_free = inner(freedom_w, 0, 1)
    opening = jnp.where(leading, inner(initial_w, 0, 1), opening)
    opening = opening + near_free * inner(fine[1], 0, 1)
    return sweep(cells, opening, mobility_w, rate_w, near_free, forcing_w)


def solution(mesh):
    cells = P("space", None, None)
    times = P("tm", "space", None, None)
    return jax.shard_map(
        on_device,
        mesh=mesh,
        in_specs=(times, cells, cells, cells, cells, P()),
        out_specs=times,
        check_vma=False,
    )
```

```python
import functools

import jax
import jax.numpy as jnp
from jax import lax
from jax.experimental import pallas as pl
from jax.experimental.pallas import tpu as pltpu
from jax.sharding import PartitionSpec as P

PASSES = 4
DAMPING = 0.8
LATERAL = 0.06
AXIAL = 0.12
STEPS = 4
SLAB = 4
EDGE = 8

VMEM = pl.BlockSpec(memory_space=pltpu.VMEM)
SMEM = pl.BlockSpec(memory_space=pltpu.SMEM)

P_INIT, P_MOB, P_FREE, P_KAP, PARCEL = 12, 16, 20, 24, 27


def shifted(values, by, axis):
    size = values.shape[axis]
    return pltpu.roll(values, by % size, axis)


def parcel_kernel(who, rates, source, initial, mobility, labels, electrode, far, near, kappa, free):
    odd = who[0]

    @pl.loop(0, SLAB)
    def _(p):
        kind = labels[p]
        value = jnp.zeros(kind.shape, jnp.float32)
        for n in range(rates.shape[0]):
            value = jnp.where(kind == n, rates[n], value)
        kappa[p] = value
        open_cell = 1.0 - electrode[p].astype(jnp.float32)
        free[p] = open_cell
        for out in (far, near):
            out[P_INIT + p] = initial[p]
            out[P_MOB + p] = mobility[p]
            out[P_FREE + p] = open_cell

    for out, begin in ((far, odd), (near, 1 - odd)):

        @pl.loop(0, SLAB - 1)
        def _(j):
            out[P_KAP + j] = kappa[begin + j]
            for t in range(STEPS):
                out[3 * t + j] = 0.5 * source[t, begin + j]


def load_static(odd, source, initial, mobility, kappa, free, far, near, force, begin, mob, kap, open_cell):
    rows = pl.ds(EDGE, mobility.shape[1])

    @pl.loop(0, SLAB)
    def _(p):
        begin[4 + p] = initial[p]
        mob[4 + p, rows] = mobility[p]
        open_cell[4 + p] = free[p]
        kap[3 + p] = kappa[p]
        for t in range(STEPS):
            force[t, 3 + p] = 0.5 * source[t, p]
        for block, wide in ((far, 8 * odd), (near, 8 - 8 * odd)):
            begin[wide + p] = block[P_INIT + p]
            mob[wide + p, rows] = block[P_MOB + p]
            open_cell[wide + p] = block[P_FREE + p]

    @pl.loop(0, SLAB - 1)
    def _(p):
        for block, wide in ((far, 7 * odd), (near, 7 - 7 * odd)):
            kap[wide + p] = block[P_KAP + p]
            for t in range(STEPS):
                force[t, wide + p] = block[3 * t + p]

    zero = jnp.zeros((EDGE, mob.shape[2]), jnp.float32)

    @pl.loop(0, mob.shape[0])
    def _(p):
        mob[p, pl.ds(0, EDGE)] = zero
        mob[p, pl.ds(mob.shape[1] - EDGE, EDGE)] = zero


def make_weights(mob, weights, first, last):
    height = mob.shape[1] - 2 * EDGE

    @pl.loop(first, last)
    def _(j):
        for r in range(0, height, 8):
            at = lambda p, d: mob[p, pl.ds(EDGE + r + d, 8)]
            here = at(j + 1, 0)
            lane = lax.broadcasted_iota(jnp.int32, here.shape, 1)
            lowest, highest = lane == 0, lane == here.shape[1] - 1
            xl = 0.5 * (here + at(j, 0))
            xh = 0.5 * (here + at(j + 2, 0))
            yl = 0.5 * (here + at(j + 1, -1))
            yh = 0.5 * (here + at(j + 1, 1))
            zl = 0.5 * (here + jnp.where(lowest, 0.0, shifted(here, 1, 1)))
            zh = 0.5 * (here + jnp.where(highest, 0.0, shifted(here, -1, 1)))
            rows = pl.ds(r, 8)
            weights[j, 0, rows] = xl
            weights[j, 1, rows] = xh
            weights[j, 2, rows] = yl
            weights[j, 3, rows] = yh
            weights[j, 4, rows] = jnp.where(lowest, 0.0, 1.5 * zl)
            weights[j, 5, rows] = jnp.where(highest, 0.0, zh)
            weights[j, 6, rows] = 1.0 + (xl + xh + yl + yh + zl + zh) + 0.5 * zh


def clear_edges(cells):
    zero = jnp.zeros((EDGE, cells.shape[-1]), jnp.float32)
    for b in range(cells.shape[0]):
        for t in range(STEPS):

            @pl.loop(0, cells.shape[2])
            def _(p):
                cells[b, t, p, pl.ds(0, EDGE)] = zero
                cells[b, t, p, pl.ds(cells.shape[3] - EDGE, EDGE)] = zero


def gathered(w, cells, b, t, p, r):
    here = cells[b, t, p, pl.ds(EDGE + r, 8)]
    total = w[0] * cells[b, t, p - 1, pl.ds(EDGE + r, 8)]
    total += w[1] * cells[b, t, p + 1, pl.ds(EDGE + r, 8)]
    total += w[2] * cells[b, t, p, pl.ds(EDGE + r - 1, 8)]
    total += w[3] * cells[b, t, p, pl.ds(EDGE + r + 1, 8)]
    total += w[4] * shifted(here, 1, 1)
    total += w[5] * shifted(here, -1, 1)
    return here, total


def run_sweep(cells, weights, kap, open_cell, force, opening):
    height = cells.shape[3] - 2 * EDGE

    @pl.loop(0, PASSES)
    def _(number):
        b = number % 2

        @pl.loop(number, 10 - number)
        def _(j):
            for r in range(0, height, 8):
                rows = pl.ds(r, 8)
                w = [weights[j, n, rows] for n in range(7)]
                rate = kap[j, rows]
                gain = DAMPING * open_cell[j + 1, rows]
                former = opening[j, rows]
                for t in range(STEPS):
                    here, total = gathered(w, cells, b, t, j + 1, r)
                    pull = rate * jnp.abs(here)
                    residue = force[t, j, rows] + former + total - here * (w[6] + 0.5 * pull)
                    cells[1 - b, t, j + 1, pl.ds(EDGE + r, 8)] = here + gain * residue / (w[6] + pull)
                    former = here


def halved(read):
    return 0.25 * ((read(0, 0) + read(0, 1)) + (read(1, 0) + read(1, 1)))


def first_kernel(who, source, initial, mobility, kappa, free, far, near, to_far, to_near, rough_out,
                 force, begin, mob, kap, open_cell, weights, cells):
    odd = who[0]
    height = mobility.shape[1]
    load_static(odd, source, initial, mobility, kappa, free, far, near, force, begin, mob, kap, open_cell)
    make_weights(mob, weights, 0, 10)
    clear_edges(cells)

    @pl.loop(0, 12)
    def _(p):
        value = begin[p]
        for t in range(STEPS):
            cells[0, t, p, pl.ds(EDGE, height)] = value

    run_sweep(cells, weights, kap, open_cell, force, begin.at[pl.ds(1, 10)])
    half = height // 2
    for a in range(6):
        rough_out[a] = halved(lambda x, y: mob[2 * a + x, pl.ds(EDGE + y, half, stride=2)])
    for out, base in ((to_far, 4 - 4 * odd), (to_near, 4 * odd)):
        for t in range(STEPS):
            for p in range(SLAB):
                out[4 * t + p] = cells[0, t, 4 + p, pl.ds(EDGE, height)]
        out[16, pl.ds(0, half)] = rough_out[base]
        out[16, pl.ds(half, half)] = rough_out[base + 1]


def residual_kernel(who, source, initial, mobility, kappa, free, far, near, own, low_far, low_near,
                    both, closing, force, begin, mob, kap, open_cell, weights, cells, residues):
    odd, leading, place, count = who[0], who[1], who[2], who[3]
    height = mobility.shape[1]
    half = height // 2
    load_static(odd, source, initial, mobility, kappa, free, far, near, force, begin, mob, kap, open_cell)
    make_weights(mob, weights, 1, 9)
    clear_edges(cells)
    rows = pl.ds(EDGE, height)
    for t in range(STEPS):

        @pl.loop(0, SLAB)
        def _(p):
            cells[0, t, 4 + p, rows] = own[4 * t + p]
            cells[0, t, 8 * odd + p, rows] = low_far[4 * t + p]
            cells[0, t, 8 - 8 * odd + p, rows] = low_near[4 * t + p]

    @pl.loop(1, 9)
    def _(j):
        for r in range(0, height, 8):
            rows = pl.ds(r, 8)
            w = [weights[j, n, rows] for n in range(7)]
            rate = kap[j, rows]
            former = jnp.where(leading == 1, begin[j + 1, rows], 0.0)
            acc = jnp.zeros_like(former)
            for t in range(STEPS):
                here, total = gathered(w, cells, 0, t, j + 1, r)
                pull = rate * jnp.abs(here)
                acc += force[t, j, rows] + former + total - here * (w[6] + 0.5 * pull)
                former = here
            residues[j - 1, rows] = acc

    for a in range(4):
        coarse = 2 * place - 1 + a
        inside = jnp.logical_and(coarse >= 0, coarse < 2 * count)
        value = halved(lambda x, y: residues[2 * a + x, pl.ds(y, half, stride=2)])
        both[0, a] = jnp.where(inside, value, 0.0)
        both[1, a] = halved(lambda x, y: cells[0, STEPS - 1, 2 + 2 * a + x, pl.ds(EDGE + y, half, stride=2)])

    @pl.loop(0, 10)
    def _(j):
        closing[j] = cells[0, STEPS - 1, j + 1, pl.ds(EDGE, height)]


def last_kernel(who, source, initial, mobility, kappa, free, far, near, own, low_far, low_near, arriving, correction,
                out, force, begin, mob, kap, open_cell, weights, cells, opening):
    odd, leading = who[0], who[1]
    height = mobility.shape[1]
    half = height // 2
    load_static(odd, source, initial, mobility, kappa, free, far, near, force, begin, mob, kap, open_cell)
    make_weights(mob, weights, 0, 10)
    clear_edges(cells)
    for y in range(2):
        rows = pl.ds(y, half, stride=2)
        into = pl.ds(EDGE + y, half, stride=2)

        @pl.loop(0, SLAB)
        def _(p):
            for block, at in ((own, 4), (low_far, 8 * odd), (low_near, 8 - 8 * odd)):
                plane = at + p
                change = open_cell[plane, rows] * correction[0, plane // 2]
                for t in range(STEPS):
                    cells[0, t, plane, into] = block[4 * t + p, rows] + change

        @pl.loop(0, 10)
        def _(j):
            base = jnp.where(leading == 1, begin[j + 1, rows], arriving[j, rows])
            opening[j, rows] = base + open_cell[j + 1, rows] * correction[1, (j + 1) // 2]

    run_sweep(cells, weights, kap, open_cell, force, opening)
    for t in range(STEPS):
        for p in range(SLAB):
            out[t, p] = cells[0, t, 4 + p, pl.ds(EDGE, height)]


def windows(height, depth):
    plane = (height, depth)
    tall = (height + 2 * EDGE, depth)
    f32 = jnp.float32
    return [
        pltpu.VMEM((STEPS, 10) + plane, f32),
        pltpu.VMEM((12,) + plane, f32),
        pltpu.VMEM((12,) + tall, f32),
        pltpu.VMEM((10,) + plane, f32),
        pltpu.VMEM((12,) + plane, f32),
        pltpu.VMEM((10, 7) + plane, f32),
    ]


def call(kernel, name, inputs, outputs, scratch, scalars=1):
    return pl.pallas_call(
        kernel,
        out_shape=[jax.ShapeDtypeStruct(o, jnp.float32) for o in outputs],
        in_specs=[SMEM] * scalars + [VMEM] * (len(inputs) - scalars),
        out_specs=[VMEM] * len(outputs),
        scratch_shapes=scratch,
        name=name,
        compiler_params=pltpu.CompilerParams(vmem_limit_bytes=28 << 20),
    )(*inputs)


def inner(values, dim, cut):
    return lax.slice_in_dim(values, cut, values.shape[dim] - cut, axis=dim)


class Coupling:
    def __init__(self, mob, inside):
        centre = mob[1:-1]
        padded = jnp.pad(centre, ((0, 0), (1, 1), (1, 1)))
        keep = inside[1:-1, None, None]
        half = 0.5 * LATERAL * keep
        axial = 0.5 * AXIAL * keep
        self.xl = half * (centre + mob[:-2])
        self.xh = half * (centre + mob[2:])
        self.yl = half * (centre + padded[:, :-2, 1:-1])
        self.yh = half * (centre + padded[:, 2:, 1:-1])
        self.zl = axial * (centre + padded[:, 1:-1, :-2])
        self.zh = axial * (centre + padded[:, 1:-1, 2:])
        self.own = keep - (self.xl + self.xh + self.yl + self.yh + self.zl + self.zh)

    def step(self, values):
        planes = values.shape[-3] - 2
        cut = (self.own.shape[0] - planes) // 2
        take = lambda w: inner(w, 0, cut)
        centre = values[..., 1:-1, :, :]
        pads = [(0, 0)] * (values.ndim - 2) + [(1, 1), (1, 1)]
        padded = jnp.pad(centre, pads)
        return (
            take(self.own) * centre
            + take(self.xl) * values[..., :-2, :, :]
            + take(self.xh) * values[..., 2:, :, :]
            + take(self.yl) * padded[..., :-2, 1:-1]
            + take(self.yh) * padded[..., 2:, 1:-1]
            + take(self.zl) * padded[..., 1:-1, :-2]
            + take(self.zh) * padded[..., 1:-1, 2:]
        )

    def steps(self, values, count):
        for number in range(count):
            values = self.step(values)
        return values


def traded(far, near):
    count = lax.axis_size("space")
    far_pairs = [(i, i + 1 if i % 2 else i - 1) for i in range(1, count - 1)]
    near_pairs = [(i, i ^ 1) for i in range(count)]
    return lax.ppermute(far, "space", far_pairs), lax.ppermute(near, "space", near_pairs)


def by_side(odd, far, near):
    return jnp.where(odd, near, far), jnp.where(odd, far, near)


def arrived(value, steps, shift=0):
    times = lax.axis_size("tm")
    count = lax.axis_size("space")
    if shift == 0:
        return lax.ppermute(value, "tm", [(k, k + steps) for k in range(times - steps)])
    pairs = [
        (k * count + s + shift, (k + steps) * count + s)
        for k in range(times - steps)
        for s in range(count)
        if 0 <= s + shift < count
    ]
    return lax.ppermute(value, ("tm", "space"), pairs)


def on_device(source, initial, mobility, labels, electrode, rates):
    _, height, depth = initial.shape
    plane = (height, depth)
    place = lax.axis_index("space")
    odd = place % 2
    leading = lax.axis_index("tm") == 0
    who = jnp.stack([odd, leading.astype(jnp.int32), place, jnp.int32(lax.axis_size("space"))]).astype(jnp.int32)
    inside = lambda reach: (
        (2 * place + jnp.arange(-reach, 2 + reach) >= 0)
        & (2 * place + jnp.arange(-reach, 2 + reach) < 2 * lax.axis_size("space"))
    ).astype(jnp.float32)

    far, near, kappa, free = call(
        parcel_kernel,
        "parcel",
        (who, rates, source, initial, mobility, labels, electrode),
        [(PARCEL,) + plane] * 2 + [initial.shape] * 2,
        [],
        2,
    )
    far, near = traded(far, near)
    static = (who, source, initial, mobility, kappa, free, far, near)
    tall = (height + 2 * EDGE, depth)

    coarse = (height // 2, depth)
    to_far, to_near, rough = call(
        first_kernel,
        "first",
        static,
        [(17,) + plane] * 2 + [(6,) + coarse],
        windows(height, depth) + [pltpu.VMEM((2, STEPS, 12) + tall, jnp.float32)],
    )
    got_far, got_near = traded(to_far, to_near)
    states = (to_far, got_far, got_near)

    both, closing = call(
        residual_kernel,
        "residual",
        static + states,
        [(2, 4) + coarse, (10,) + plane],
        windows(height, depth)
        + [pltpu.VMEM((1, STEPS, 12) + tall, jnp.float32), pltpu.VMEM((8,) + plane, jnp.float32)],
    )
    rough_of = lambda b: b[16].reshape((2,) + coarse)
    low, high = by_side(odd == 1, rough_of(got_far), rough_of(got_near))
    rough_w = jnp.concatenate([low, rough, high], axis=0)

    one = arrived(both, 1)
    two = arrived(both, 2)
    three = arrived(both[1], 3)
    rhs = both[0] + one[1]
    rhs1 = one[0] + two[1]
    rhs2 = two[0] + three
    pair = jnp.stack([inner(rhs, 0, 1), inner(rhs1, 0, 1)])
    pair = pair + Coupling(inner(rough_w, 0, 3), inside(1)).step(jnp.stack([rhs1, rhs2]))

    cargo = lambda c: jnp.concatenate([pair.reshape((4,) + coarse), c], axis=0)
    to_low, to_high = cargo(rough_w[8:10]), cargo(rough_w[0:2])
    low, high = by_side(odd == 1, *traded(*by_side(odd == 1, to_low, to_high)))
    opening = arrived(closing, 1)
    pair_of = lambda b: b[:4].reshape(pair.shape)
    rough_far = jnp.concatenate([low[4:], rough_w, high[4:]], axis=0)
    pair = jnp.concatenate([pair_of(low), pair, pair_of(high)], axis=1)
    low, high = arrived(pair, 2, -1), arrived(pair, 2, 1)
    middle = jnp.where(place == 0, high[:, :2], low[:, 4:])
    older = jnp.concatenate([low[:, :4], middle, high[:, 2:]], axis=1)
    coupling = Coupling(rough_far, inside(6))
    pair = pair + coupling.steps(older, 2)
    older = jnp.concatenate([arrived(pair[:, :4], 4, -2), arrived(pair, 4), arrived(pair[:, 2:], 4, 2)], axis=1)
    correction = pair + coupling.steps(older, 4)

    (density,) = call(
        last_kernel,
        "last",
        static + states + (opening, correction),
        [source.shape],
        windows(height, depth)
        + [pltpu.VMEM((2, STEPS, 12) + tall, jnp.float32), pltpu.VMEM((10,) + plane, jnp.float32)],
    )
    return density


def solution(mesh):
    cells = P("space", None, None)
    times = P("tm", "space", None, None)
    return jax.shard_map(
        on_device,
        mesh=mesh,
        in_specs=(times, cells, cells, cells, cells, P()),
        out_specs=times,
        check_vma=False,
    )
```

```python
import jax
import jax.numpy as jnp
from jax import lax
from jax.experimental import pallas as pl
from jax.experimental.pallas import tpu as pltpu
from jax.sharding import PartitionSpec as P

PASSES = 4
DAMPING = 0.8
LATERAL = 0.06
AXIAL = 0.12
STEPS = 4
SLAB = 4
EDGE = 8

VMEM = pl.BlockSpec(memory_space=pltpu.VMEM)
SMEM = pl.BlockSpec(memory_space=pltpu.SMEM)

P_INIT, P_MOB, P_FREE, P_KAP, PARCEL = 12, 16, 20, 24, 27
O_INIT, O_MOB, O_FREE, O_KAP, OWN = 16, 20, 24, 28, 32


def shifted(values, by, axis):
    size = values.shape[axis]
    return pltpu.roll(values, by % size, axis)


def parcel_kernel(who, rates, source, initial, mobility, labels, electrode, far, near, own):
    odd = who[0]

    @pl.loop(0, SLAB)
    def _(p):
        kind = labels[p]
        value = jnp.zeros(kind.shape, jnp.float32)
        for n in range(rates.shape[0]):
            value = jnp.where(kind == n, rates[n], value)
        own[O_KAP + p] = value
        open_cell = 1.0 - electrode[p].astype(jnp.float32)
        own[O_FREE + p] = open_cell
        own[O_INIT + p] = initial[p]
        own[O_MOB + p] = mobility[p]
        for t in range(STEPS):
            own[SLAB * t + p] = 0.5 * source[t, p]
        for out in (far, near):
            out[P_INIT + p] = initial[p]
            out[P_MOB + p] = mobility[p]
            out[P_FREE + p] = open_cell

    for out, begin in ((far, odd), (near, 1 - odd)):

        @pl.loop(0, SLAB - 1)
        def _(j):
            out[P_KAP + j] = own[O_KAP + begin + j]
            for t in range(STEPS):
                out[3 * t + j] = own[SLAB * t + begin + j]


def load_static(odd, fixed, far, near, force, begin, mob, kap, open_cell):
    rows = pl.ds(EDGE, fixed.shape[1])

    @pl.loop(0, SLAB)
    def _(p):
        begin[4 + p] = fixed[O_INIT + p]
        mob[4 + p, rows] = fixed[O_MOB + p]
        open_cell[4 + p] = fixed[O_FREE + p]
        kap[3 + p] = fixed[O_KAP + p]
        for t in range(STEPS):
            force[t, 3 + p] = fixed[SLAB * t + p]
        for block, wide in ((far, 8 * odd), (near, 8 - 8 * odd)):
            begin[wide + p] = block[P_INIT + p]
            mob[wide + p, rows] = block[P_MOB + p]
            open_cell[wide + p] = block[P_FREE + p]

    @pl.loop(0, SLAB - 1)
    def _(p):
        for block, wide in ((far, 7 * odd), (near, 7 - 7 * odd)):
            kap[wide + p] = block[P_KAP + p]
            for t in range(STEPS):
                force[t, wide + p] = block[3 * t + p]

    zero = jnp.zeros((EDGE, mob.shape[2]), jnp.float32)

    @pl.loop(0, mob.shape[0])
    def _(p):
        mob[p, pl.ds(0, EDGE)] = zero
        mob[p, pl.ds(mob.shape[1] - EDGE, EDGE)] = zero


def make_weights(mob, weights, first, last):
    height = mob.shape[1] - 2 * EDGE

    @pl.loop(first, last)
    def _(j):
        for r in range(0, height, 8):
            at = lambda p, d: mob[p, pl.ds(EDGE + r + d, 8)]
            here = at(j + 1, 0)
            lane = lax.broadcasted_iota(jnp.int32, here.shape, 1)
            lowest, highest = lane == 0, lane == here.shape[1] - 1
            xl = 0.5 * (here + at(j, 0))
            xh = 0.5 * (here + at(j + 2, 0))
            yl = 0.5 * (here + at(j + 1, -1))
            yh = 0.5 * (here + at(j + 1, 1))
            zl = 0.5 * (here + jnp.where(lowest, 0.0, shifted(here, 1, 1)))
            zh = 0.5 * (here + jnp.where(highest, 0.0, shifted(here, -1, 1)))
            rows = pl.ds(r, 8)
            weights[j, 0, rows] = xl
            weights[j, 1, rows] = xh
            weights[j, 2, rows] = yl
            weights[j, 3, rows] = yh
            weights[j, 4, rows] = jnp.where(lowest, 0.0, 1.5 * zl)
            weights[j, 5, rows] = jnp.where(highest, 0.0, zh)
            weights[j, 6, rows] = 1.0 + (xl + xh + yl + yh + zl + zh) + 0.5 * zh


def clear_edges(cells):
    zero = jnp.zeros((EDGE, cells.shape[-1]), jnp.float32)

    @pl.loop(0, cells.shape[1])
    def _(p):
        for t in range(STEPS):
            cells[t, p, pl.ds(0, EDGE)] = zero
            cells[t, p, pl.ds(cells.shape[2] - EDGE, EDGE)] = zero


def gathered(w, cells, t, p, r):
    here = cells[t, p, pl.ds(EDGE + r, 8)]
    total = w[0] * cells[t, p - 1, pl.ds(EDGE + r, 8)]
    total += w[1] * cells[t, p + 1, pl.ds(EDGE + r, 8)]
    total += w[2] * cells[t, p, pl.ds(EDGE + r - 1, 8)]
    total += w[3] * cells[t, p, pl.ds(EDGE + r + 1, 8)]
    total += w[4] * shifted(here, 1, 1)
    total += w[5] * shifted(here, -1, 1)
    return here, total


def run_sweep(cells, other, weights, kap, open_cell, force, opening):
    height = cells.shape[2] - 2 * EDGE
    for number in range(PASSES):
        source, target = (cells, other) if number % 2 == 0 else (other, cells)

        @pl.loop(number, 10 - number)
        def _(j):
            for r in range(0, height, 8):
                rows = pl.ds(r, 8)
                w = [weights[j, n, rows] for n in range(7)]
                rate = kap[j, rows]
                gain = DAMPING * open_cell[j + 1, rows]
                former = opening[j, rows]
                for t in range(STEPS):
                    here, total = gathered(w, source, t, j + 1, r)
                    pull = rate * jnp.abs(here)
                    residue = force[t, j, rows] + former + total - here * (w[6] + 0.5 * pull)
                    target[t, j + 1, pl.ds(EDGE + r, 8)] = here + gain * residue / (w[6] + pull)
                    former = here


def halved(read):
    return 0.25 * ((read(0, 0) + read(0, 1)) + (read(1, 0) + read(1, 1)))


def first_kernel(who, fixed, far, near, to_far, to_near, rough_out, closing,
                 force, begin, mob, kap, open_cell, weights, cells, other):
    odd = who[0]
    height = fixed.shape[1]
    load_static(odd, fixed, far, near, force, begin, mob, kap, open_cell)
    make_weights(mob, weights, 0, 10)
    clear_edges(cells)

    @pl.loop(0, 12)
    def _(p):
        value = begin[p]
        for t in range(STEPS):
            cells[t, p, pl.ds(EDGE, height)] = value

    clear_edges(other)
    run_sweep(cells, other, weights, kap, open_cell, force, begin.at[pl.ds(1, 10)])
    for p in range(SLAB):
        closing[p] = cells[STEPS - 1, 4 + p, pl.ds(EDGE, height)]
    half = height // 2
    for a in range(6):
        rough_out[a] = halved(lambda x, y: mob[2 * a + x, pl.ds(EDGE + y, half, stride=2)])
    for out, base in ((to_far, 4 - 4 * odd), (to_near, 4 * odd)):
        for t in range(STEPS):
            for p in range(SLAB):
                out[4 * t + p] = cells[t, 4 + p, pl.ds(EDGE, height)]
        out[16, pl.ds(0, half)] = rough_out[base]
        out[16, pl.ds(half, half)] = rough_out[base + 1]


def residual_kernel(who, fixed, far, near, own, low_far, low_near,
                    both, force, begin, mob, kap, open_cell, weights, cells, residues):
    odd, leading, place, count = who[0], who[1], who[2], who[3]
    height = fixed.shape[1]
    half = height // 2
    load_static(odd, fixed, far, near, force, begin, mob, kap, open_cell)
    make_weights(mob, weights, 1, 9)
    clear_edges(cells)
    rows = pl.ds(EDGE, height)
    for t in range(STEPS):

        @pl.loop(0, SLAB)
        def _(p):
            cells[t, 4 + p, rows] = own[4 * t + p]
            cells[t, 8 * odd + p, rows] = low_far[4 * t + p]
            cells[t, 8 - 8 * odd + p, rows] = low_near[4 * t + p]

    @pl.loop(1, 9)
    def _(j):
        for r in range(0, height, 8):
            rows = pl.ds(r, 8)
            w = [weights[j, n, rows] for n in range(7)]
            rate = kap[j, rows]
            former = jnp.where(leading == 1, begin[j + 1, rows], 0.0)
            acc = jnp.zeros_like(former)
            for t in range(STEPS):
                here, total = gathered(w, cells, t, j + 1, r)
                pull = rate * jnp.abs(here)
                acc += force[t, j, rows] + former + total - here * (w[6] + 0.5 * pull)
                former = here
            residues[j - 1, rows] = acc

    for a in range(4):
        coarse = 2 * place - 1 + a
        inside = jnp.logical_and(coarse >= 0, coarse < 2 * count)
        value = halved(lambda x, y: residues[2 * a + x, pl.ds(y, half, stride=2)])
        both[0, a] = jnp.where(inside, value, 0.0)
        both[1, a] = halved(lambda x, y: cells[STEPS - 1, 2 + 2 * a + x, pl.ds(EDGE + y, half, stride=2)])


def last_kernel(who, fixed, far, near, own, low_far, low_near, arriving, side_far, side_near, correction,
                out, force, begin, mob, kap, open_cell, weights, cells, other, opening):
    odd, leading = who[0], who[1]
    height = fixed.shape[1]
    half = height // 2
    load_static(odd, fixed, far, near, force, begin, mob, kap, open_cell)
    make_weights(mob, weights, 0, 10)
    clear_edges(cells)
    for y in range(2):
        rows = pl.ds(y, half, stride=2)
        into = pl.ds(EDGE + y, half, stride=2)

        @pl.loop(0, SLAB)
        def _(p):
            for block, at in ((own, 4), (low_far, 8 * odd), (low_near, 8 - 8 * odd)):
                plane = at + p
                change = open_cell[plane, rows] * correction[0, plane // 2]
                for t in range(STEPS):
                    cells[t, plane, into] = block[4 * t + p, rows] + change

        def enter(j, value):
            base = jnp.where(leading == 1, begin[j + 1, rows], value)
            opening[j, rows] = base + open_cell[j + 1, rows] * correction[1, (j + 1) // 2]

        @pl.loop(0, SLAB)
        def _(p):
            enter(3 + p, arriving[p, rows])

        @pl.loop(0, SLAB - 1)
        def _(p):
            enter(7 * odd + p, side_far[3 + p, rows])
            enter(7 - 7 * odd + p, side_near[3 + p, rows])

    clear_edges(other)
    run_sweep(cells, other, weights, kap, open_cell, force, opening)
    for t in range(STEPS):
        for p in range(SLAB):
            out[t, p] = cells[t, 4 + p, pl.ds(EDGE, height)]


def windows(height, depth):
    plane = (height, depth)
    tall = (height + 2 * EDGE, depth)
    f32 = jnp.float32
    return [
        pltpu.VMEM((STEPS, 10) + plane, f32),
        pltpu.VMEM((12,) + plane, f32),
        pltpu.VMEM((12,) + tall, f32),
        pltpu.VMEM((10,) + plane, f32),
        pltpu.VMEM((12,) + plane, f32),
        pltpu.VMEM((10, 7) + plane, f32),
    ]


def call(kernel, name, inputs, outputs, scratch, scalars=1, grant=28):
    return pl.pallas_call(
        kernel,
        out_shape=[jax.ShapeDtypeStruct(o, jnp.float32) for o in outputs],
        in_specs=[SMEM] * scalars + [VMEM] * (len(inputs) - scalars),
        out_specs=[VMEM] * len(outputs),
        scratch_shapes=scratch,
        name=name,
        compiler_params=pltpu.CompilerParams(vmem_limit_bytes=grant << 20),
    )(*inputs)


def inner(values, dim, cut):
    return lax.slice_in_dim(values, cut, values.shape[dim] - cut, axis=dim)


class Coupling:
    def __init__(self, mob, inside):
        centre = mob[1:-1]
        padded = jnp.pad(centre, ((0, 0), (1, 1), (1, 1)))
        keep = inside[1:-1, None, None]
        half = 0.5 * LATERAL * keep
        axial = 0.5 * AXIAL * keep
        self.xl = half * (centre + mob[:-2])
        self.xh = half * (centre + mob[2:])
        self.yl = half * (centre + padded[:, :-2, 1:-1])
        self.yh = half * (centre + padded[:, 2:, 1:-1])
        self.zl = axial * (centre + padded[:, 1:-1, :-2])
        self.zh = axial * (centre + padded[:, 1:-1, 2:])
        self.own = keep - (self.xl + self.xh + self.yl + self.yh + self.zl + self.zh)

    def step(self, values):
        planes = values.shape[-3] - 2
        cut = (self.own.shape[0] - planes) // 2
        take = lambda w: inner(w, 0, cut)
        centre = values[..., 1:-1, :, :]
        pads = [(0, 0)] * (values.ndim - 2) + [(1, 1), (1, 1)]
        padded = jnp.pad(centre, pads)
        return (
            take(self.own) * centre
            + take(self.xl) * values[..., :-2, :, :]
            + take(self.xh) * values[..., 2:, :, :]
            + take(self.yl) * padded[..., :-2, 1:-1]
            + take(self.yh) * padded[..., 2:, 1:-1]
            + take(self.zl) * padded[..., 1:-1, :-2]
            + take(self.zh) * padded[..., 1:-1, 2:]
        )

    def steps(self, values, count):
        for number in range(count):
            values = self.step(values)
        return values


def traded(far, near, steps=0):
    times = lax.axis_size("tm")
    count = lax.axis_size("space")
    far_of = [i + 1 if i % 2 else i - 1 for i in range(count)]
    near_of = [i ^ 1 for i in range(count)]

    def send(value, to):
        pairs = [
            (k * count + i, (k + steps) * count + to[i])
            for k in range(times - steps)
            for i in range(count)
            if 0 <= to[i] < count
        ]
        return lax.ppermute(value, ("tm", "space"), pairs)

    return send(far, far_of), send(near, near_of)


def by_side(odd, far, near):
    return jnp.where(odd, near, far), jnp.where(odd, far, near)


def arrived(value, steps, shift=0):
    times = lax.axis_size("tm")
    count = lax.axis_size("space")
    if shift == 0:
        return lax.ppermute(value, "tm", [(k, k + steps) for k in range(times - steps)])
    pairs = [
        (k * count + s + shift, (k + steps) * count + s)
        for k in range(times - steps)
        for s in range(count)
        if 0 <= s + shift < count
    ]
    return lax.ppermute(value, ("tm", "space"), pairs)


def on_device(source, initial, mobility, labels, electrode, rates):
    _, height, depth = initial.shape
    plane = (height, depth)
    place = lax.axis_index("space")
    odd = place % 2
    leading = lax.axis_index("tm") == 0
    who = jnp.stack([odd, leading.astype(jnp.int32), place, jnp.int32(lax.axis_size("space"))]).astype(jnp.int32)
    inside = lambda reach: (
        (2 * place + jnp.arange(-reach, 2 + reach) >= 0)
        & (2 * place + jnp.arange(-reach, 2 + reach) < 2 * lax.axis_size("space"))
    ).astype(jnp.float32)

    far, near, fixed = call(
        parcel_kernel,
        "parcel",
        (who, rates, source, initial, mobility, labels, electrode),
        [(PARCEL,) + plane] * 2 + [(OWN,) + plane],
        [],
        2,
        60,
    )
    far, near = traded(far, near)
    static = (who, fixed, far, near)
    tall = (height + 2 * EDGE, depth)

    coarse = (height // 2, depth)
    to_far, to_near, rough, closing = call(
        first_kernel,
        "first",
        static,
        [(17,) + plane] * 2 + [(6,) + coarse, initial.shape],
        windows(height, depth) + [pltpu.VMEM((STEPS, 12) + tall, jnp.float32)] * 2,
    )
    got_far, got_near = traded(to_far, to_near)
    opening = arrived(closing, 1)
    states = (to_far, got_far, got_near)

    (both,) = call(
        residual_kernel,
        "residual",
        static + states,
        [(2, 4) + coarse],
        windows(height, depth)
        + [pltpu.VMEM((STEPS, 12) + tall, jnp.float32), pltpu.VMEM((8,) + plane, jnp.float32)],
    )
    rough_of = lambda b: b[16].reshape((2,) + coarse)
    low, high = by_side(odd == 1, rough_of(got_far), rough_of(got_near))
    rough_w = jnp.concatenate([low, rough, high], axis=0)

    one = arrived(both, 1)
    two = arrived(both, 2)
    three = arrived(both[1], 3)
    rhs = both[0] + one[1]
    rhs1 = one[0] + two[1]
    rhs2 = two[0] + three
    pair = jnp.stack([inner(rhs, 0, 1), inner(rhs1, 0, 1)])
    pair = pair + Coupling(inner(rough_w, 0, 3), inside(1)).step(jnp.stack([rhs1, rhs2]))

    flat = lambda v: v.reshape((-1,) + plane)
    unflat = lambda v: v.reshape((-1,) + coarse)
    cargo = lambda c, o: jnp.concatenate([flat(pair), flat(c), o], axis=0)
    to_low = cargo(rough_w[8:10], opening[: SLAB - 1])
    to_high = cargo(rough_w[0:2], opening[1:])
    side_far, side_near = traded(*by_side(odd == 1, to_low, to_high))
    low, high = by_side(odd == 1, unflat(side_far[:3]), unflat(side_near[:3]))
    pair_of = lambda b: b[:4].reshape(pair.shape)
    rough_far = jnp.concatenate([low[4:], rough_w, high[4:]], axis=0)
    pair = jnp.concatenate([pair_of(low), pair, pair_of(high)], axis=1)
    low, high = by_side(odd == 1, *traded(pair, pair, 2))
    middle = jnp.where(place == 0, high[:, :2], low[:, 4:])
    older = jnp.concatenate([low[:, :4], middle, high[:, 2:]], axis=1)
    coupling = Coupling(rough_far, inside(6))
    pair = pair + coupling.steps(older, 2)
    older = jnp.concatenate([arrived(pair[:, :4], 4, -2), arrived(pair, 4), arrived(pair[:, 2:], 4, 2)], axis=1)
    correction = pair + coupling.steps(older, 4)

    (density,) = call(
        last_kernel,
        "last",
        static + states + (opening, side_far, side_near, correction),
        [source.shape],
        windows(height, depth)
        + [pltpu.VMEM((STEPS, 12) + tall, jnp.float32)] * 2
        + [pltpu.VMEM((10,) + plane, jnp.float32)],
    )
    return density


def solution(mesh):
    cells = P("space", None, None)
    times = P("tm", "space", None, None)
    return jax.shard_map(
        on_device,
        mesh=mesh,
        in_specs=(times, cells, cells, cells, cells, P()),
        out_specs=times,
        check_vma=False,
    )
```

```python
import jax
import jax.numpy as jnp
from jax import lax
from jax.experimental import pallas as pl
from jax.experimental.pallas import tpu as pltpu
from jax.sharding import PartitionSpec as P

PASSES = 4
DAMPING = 0.8
LATERAL = 0.06
AXIAL = 0.12
STEPS = 4
SLAB = 4
EDGE = 8

VMEM = pl.BlockSpec(memory_space=pltpu.VMEM)
SMEM = pl.BlockSpec(memory_space=pltpu.SMEM)

P_INIT, P_MOB, P_FREE, P_KAP, PARCEL = 12, 16, 20, 24, 27
O_INIT, O_MOB, O_FREE, O_KAP, OWN = 16, 20, 24, 28, 32


def shifted(values, by, axis):
    size = values.shape[axis]
    return pltpu.roll(values, by % size, axis)


def parcel_kernel(rates, source_at, initial_at, mobility_at, labels_at, electrode_at, far, near, own,
                  source, initial, mobility, labels, electrode, done):
    odd = lax.rem(lax.axis_index("space"), 2)
    places = (
        (labels_at, labels), (electrode_at, electrode), (initial_at, initial),
        (mobility_at, mobility), (source_at, source),
    )
    copies = [pltpu.make_async_copy(there, here, done.at[n]) for n, (there, here) in enumerate(places)]
    for copy in copies:
        copy.start()
    for copy in copies:
        copy.wait()

    @pl.loop(0, SLAB)
    def _(p):
        kind = labels[p]
        value = jnp.zeros(kind.shape, jnp.float32)
        for n in range(rates.shape[0]):
            value = jnp.where(kind == n, rates[n], value)
        own[O_KAP + p] = value
        open_cell = 1.0 - electrode[p].astype(jnp.float32)
        own[O_FREE + p] = open_cell
        own[O_INIT + p] = initial[p]
        own[O_MOB + p] = mobility[p]
        for t in range(STEPS):
            own[SLAB * t + p] = 0.5 * source[t, p]
        for out in (far, near):
            out[P_INIT + p] = initial[p]
            out[P_MOB + p] = mobility[p]
            out[P_FREE + p] = open_cell

    for out, begin in ((far, odd), (near, 1 - odd)):

        @pl.loop(0, SLAB - 1)
        def _(j):
            out[P_KAP + j] = own[O_KAP + begin + j]
            for t in range(STEPS):
                out[3 * t + j] = own[SLAB * t + begin + j]


def load_static(odd, fixed, far, near, force, begin, mob, kap, open_cell):
    rows = pl.ds(EDGE, fixed.shape[1])

    @pl.loop(0, SLAB)
    def _(p):
        begin[4 + p] = fixed[O_INIT + p]
        mob[4 + p, rows] = fixed[O_MOB + p]
        open_cell[4 + p] = fixed[O_FREE + p]
        kap[3 + p] = fixed[O_KAP + p]
        for t in range(STEPS):
            force[t, 3 + p] = fixed[SLAB * t + p]
        for block, wide in ((far, 8 * odd), (near, 8 - 8 * odd)):
            begin[wide + p] = block[P_INIT + p]
            mob[wide + p, rows] = block[P_MOB + p]
            open_cell[wide + p] = block[P_FREE + p]

    @pl.loop(0, SLAB - 1)
    def _(p):
        for block, wide in ((far, 7 * odd), (near, 7 - 7 * odd)):
            kap[wide + p] = block[P_KAP + p]
            for t in range(STEPS):
                force[t, wide + p] = block[3 * t + p]

    zero = jnp.zeros((EDGE, mob.shape[2]), jnp.float32)

    @pl.loop(0, mob.shape[0])
    def _(p):
        mob[p, pl.ds(0, EDGE)] = zero
        mob[p, pl.ds(mob.shape[1] - EDGE, EDGE)] = zero


def make_weights(mob, weights, first, last):
    height = mob.shape[1] - 2 * EDGE

    @pl.loop(first, last)
    def _(j):
        for r in range(0, height, 8):
            at = lambda p, d: mob[p, pl.ds(EDGE + r + d, 8)]
            here = at(j + 1, 0)
            lane = lax.broadcasted_iota(jnp.int32, here.shape, 1)
            lowest, highest = lane == 0, lane == here.shape[1] - 1
            xl = 0.5 * (here + at(j, 0))
            xh = 0.5 * (here + at(j + 2, 0))
            yl = 0.5 * (here + at(j + 1, -1))
            yh = 0.5 * (here + at(j + 1, 1))
            zl = 0.5 * (here + jnp.where(lowest, 0.0, shifted(here, 1, 1)))
            zh = 0.5 * (here + jnp.where(highest, 0.0, shifted(here, -1, 1)))
            rows = pl.ds(r, 8)
            weights[j, 0, rows] = xl
            weights[j, 1, rows] = xh
            weights[j, 2, rows] = yl
            weights[j, 3, rows] = yh
            weights[j, 4, rows] = jnp.where(lowest, 0.0, 1.5 * zl)
            weights[j, 5, rows] = jnp.where(highest, 0.0, zh)
            weights[j, 6, rows] = 1.0 + (xl + xh + yl + yh + zl + zh) + 0.5 * zh


def clear_edges(cells):
    zero = jnp.zeros((EDGE, cells.shape[-1]), jnp.float32)

    @pl.loop(0, cells.shape[1])
    def _(p):
        for t in range(STEPS):
            cells[t, p, pl.ds(0, EDGE)] = zero
            cells[t, p, pl.ds(cells.shape[2] - EDGE, EDGE)] = zero


def gathered(w, cells, t, p, r):
    here = cells[t, p, pl.ds(EDGE + r, 8)]
    total = w[0] * cells[t, p - 1, pl.ds(EDGE + r, 8)]
    total += w[1] * cells[t, p + 1, pl.ds(EDGE + r, 8)]
    total += w[2] * cells[t, p, pl.ds(EDGE + r - 1, 8)]
    total += w[3] * cells[t, p, pl.ds(EDGE + r + 1, 8)]
    total += w[4] * shifted(here, 1, 1)
    total += w[5] * shifted(here, -1, 1)
    return here, total


def run_sweep(cells, other, weights, kap, open_cell, force, opening):
    height = cells.shape[2] - 2 * EDGE
    for number in range(PASSES):
        source, target = (cells, other) if number % 2 == 0 else (other, cells)

        @pl.loop(number, 10 - number)
        def _(j):
            for r in range(0, height, 8):
                rows = pl.ds(r, 8)
                w = [weights[j, n, rows] for n in range(7)]
                rate = kap[j, rows]
                gain = DAMPING * open_cell[j + 1, rows]
                former = opening[j, rows]
                for t in range(STEPS):
                    here, total = gathered(w, source, t, j + 1, r)
                    pull = rate * jnp.abs(here)
                    residue = force[t, j, rows] + former + total - here * (w[6] + 0.5 * pull)
                    target[t, j + 1, pl.ds(EDGE + r, 8)] = here + gain * residue / (w[6] + pull)
                    former = here


def halved(read):
    return 0.25 * ((read(0, 0) + read(0, 1)) + (read(1, 0) + read(1, 1)))


def first_kernel(who, fixed, far, near, to_far, to_near, closing,
                 force, begin, mob, kap, open_cell, weights, cells, other, rough):
    odd = who[0]
    height = fixed.shape[1]
    load_static(odd, fixed, far, near, force, begin, mob, kap, open_cell)
    make_weights(mob, weights, 0, 10)
    clear_edges(cells)

    @pl.loop(0, 12)
    def _(p):
        value = begin[p]
        for t in range(STEPS):
            cells[t, p, pl.ds(EDGE, height)] = value

    clear_edges(other)
    run_sweep(cells, other, weights, kap, open_cell, force, begin.at[pl.ds(1, 10)])
    for p in range(SLAB):
        closing[p] = cells[STEPS - 1, 4 + p, pl.ds(EDGE, height)]
    half = height // 2
    for a in range(6):
        rough[a] = halved(lambda x, y: mob[2 * a + x, pl.ds(EDGE + y, half, stride=2)])
    for out, base in ((to_far, 4 - 4 * odd), (to_near, 4 * odd)):
        for t in range(STEPS):
            for p in range(SLAB):
                out[4 * t + p] = cells[t, 4 + p, pl.ds(EDGE, height)]
        out[16, pl.ds(0, half)] = rough[base]
        out[16, pl.ds(half, half)] = rough[base + 1]


def residual_kernel(who, fixed, far, near, own, low_far, low_near, arriving,
                    base, closing, both, rhs, rough, force, begin, mob, kap, open_cell, weights, cells, residues):
    odd, leading, place, count = who[0], who[1], who[2], who[3]
    height = fixed.shape[1]
    half = height // 2
    load_static(odd, fixed, far, near, force, begin, mob, kap, open_cell)
    make_weights(mob, weights, 1, 9)
    clear_edges(cells)
    rows = pl.ds(EDGE, height)
    for t in range(STEPS):

        @pl.loop(0, SLAB)
        def _(p):
            cells[t, 4 + p, rows] = own[4 * t + p]
            cells[t, 8 * odd + p, rows] = low_far[4 * t + p]
            cells[t, 8 - 8 * odd + p, rows] = low_near[4 * t + p]

    @pl.loop(1, 9)
    def _(j):
        for r in range(0, height, 8):
            rows = pl.ds(r, 8)
            w = [weights[j, n, rows] for n in range(7)]
            rate = kap[j, rows]
            former = jnp.where(leading == 1, begin[j + 1, rows], 0.0)
            acc = jnp.zeros_like(former)
            for t in range(STEPS):
                here, total = gathered(w, cells, t, j + 1, r)
                pull = rate * jnp.abs(here)
                acc += force[t, j, rows] + former + total - here * (w[6] + 0.5 * pull)
                former = here
            residues[j - 1, rows] = acc

    for a in range(4):
        coarse = 2 * place - 1 + a
        inside = jnp.logical_and(coarse >= 0, coarse < 2 * count)
        value = halved(lambda x, y: residues[2 * a + x, pl.ds(y, half, stride=2)])
        base[a] = jnp.where(inside, value, 0.0)
        closing[a] = halved(lambda x, y: cells[STEPS - 1, 2 + 2 * a + x, pl.ds(EDGE + y, half, stride=2)])
        both[0, a] = base[a]
        both[1, a] = closing[a]
    for a in range(2):
        rhs[a] = base[1 + a] + halved(lambda x, y: arriving[2 * a + x, pl.ds(y, half, stride=2)])
        for block, at in ((low_far, 8 * odd), (low_near, 8 - 8 * odd)):
            rough[at + a] = block[16, pl.ds(half * a, half)]
    for a in range(6):
        rough[2 + a] = halved(lambda x, y: mob[2 * a + x, pl.ds(EDGE + y, half, stride=2)])


def last_kernel(who, fixed, far, near, own, low_far, low_near, arriving, side_far, side_near, correction,
                out, force, begin, mob, kap, open_cell, weights, cells, other, opening):
    odd, leading = who[0], who[1]
    height = fixed.shape[1]
    half = height // 2
    load_static(odd, fixed, far, near, force, begin, mob, kap, open_cell)
    make_weights(mob, weights, 0, 10)
    clear_edges(cells)
    for y in range(2):
        rows = pl.ds(y, half, stride=2)
        into = pl.ds(EDGE + y, half, stride=2)

        @pl.loop(0, SLAB)
        def _(p):
            for block, at in ((own, 4), (low_far, 8 * odd), (low_near, 8 - 8 * odd)):
                plane = at + p
                change = open_cell[plane, rows] * correction[0, plane // 2]
                for t in range(STEPS):
                    cells[t, plane, into] = block[4 * t + p, rows] + change

        def enter(j, value):
            base = jnp.where(leading == 1, begin[j + 1, rows], value)
            opening[j, rows] = base + open_cell[j + 1, rows] * correction[1, (j + 1) // 2]

        @pl.loop(0, SLAB)
        def _(p):
            enter(3 + p, arriving[p, rows])

        @pl.loop(0, SLAB - 1)
        def _(p):
            enter(7 * odd + p, side_far[3 + p, rows])
            enter(7 - 7 * odd + p, side_near[3 + p, rows])

    clear_edges(other)
    run_sweep(cells, other, weights, kap, open_cell, force, opening)
    for t in range(STEPS):
        for p in range(SLAB):
            out[t, p] = cells[t, 4 + p, pl.ds(EDGE, height)]


def windows(height, depth):
    plane = (height, depth)
    tall = (height + 2 * EDGE, depth)
    f32 = jnp.float32
    return [
        pltpu.VMEM((STEPS, 10) + plane, f32),
        pltpu.VMEM((12,) + plane, f32),
        pltpu.VMEM((12,) + tall, f32),
        pltpu.VMEM((10,) + plane, f32),
        pltpu.VMEM((12,) + plane, f32),
        pltpu.VMEM((10, 7) + plane, f32),
    ]


def call(kernel, name, inputs, outputs, scratch):
    return pl.pallas_call(
        kernel,
        out_shape=[jax.ShapeDtypeStruct(o, jnp.float32) for o in outputs],
        in_specs=[SMEM] + [VMEM] * (len(inputs) - 1),
        out_specs=[VMEM] * len(outputs),
        scratch_shapes=scratch,
        name=name,
        compiler_params=pltpu.CompilerParams(vmem_limit_bytes=28 << 20),
    )(*inputs)


def inner(values, dim, cut):
    return lax.slice_in_dim(values, cut, values.shape[dim] - cut, axis=dim)


class Coupling:
    def __init__(self, mob, inside):
        centre = mob[1:-1]
        padded = jnp.pad(centre, ((0, 0), (1, 1), (1, 1)))
        keep = inside[1:-1, None, None]
        half = 0.5 * LATERAL * keep
        axial = 0.5 * AXIAL * keep
        self.xl = half * (centre + mob[:-2])
        self.xh = half * (centre + mob[2:])
        self.yl = half * (centre + padded[:, :-2, 1:-1])
        self.yh = half * (centre + padded[:, 2:, 1:-1])
        self.zl = axial * (centre + padded[:, 1:-1, :-2])
        self.zh = axial * (centre + padded[:, 1:-1, 2:])
        self.own = keep - (self.xl + self.xh + self.yl + self.yh + self.zl + self.zh)

    def step(self, values):
        planes = values.shape[-3] - 2
        cut = (self.own.shape[0] - planes) // 2
        take = lambda w: inner(w, 0, cut)
        centre = values[..., 1:-1, :, :]
        pads = [(0, 0)] * (values.ndim - 2) + [(1, 1), (1, 1)]
        padded = jnp.pad(centre, pads)
        return (
            take(self.own) * centre
            + take(self.xl) * values[..., :-2, :, :]
            + take(self.xh) * values[..., 2:, :, :]
            + take(self.yl) * padded[..., :-2, 1:-1]
            + take(self.yh) * padded[..., 2:, 1:-1]
            + take(self.zl) * padded[..., 1:-1, :-2]
            + take(self.zh) * padded[..., 1:-1, 2:]
        )

    def steps(self, values, count):
        for number in range(count):
            values = self.step(values)
        return values


def sent(value, steps, to):
    times = lax.axis_size("tm")
    count = lax.axis_size("space")
    pairs = [
        (k * count + i, (k + steps) * count + to[i])
        for k in range(times - steps)
        for i in range(count)
        if 0 <= to[i] < count
    ]
    return lax.ppermute(value, ("tm", "space"), pairs)


def traded(far, near):
    count = lax.axis_size("space")
    far_of = [i + 1 if i % 2 else i - 1 for i in range(count)]
    return sent(far, 0, far_of), sent(near, 0, [i ^ 1 for i in range(count)])


def by_side(odd, far, near):
    return jnp.where(odd, near, far), jnp.where(odd, far, near)


def arrived(value, steps):
    times = lax.axis_size("tm")
    return lax.ppermute(value, "tm", [(k, k + steps) for k in range(times - steps)])


def on_device(source, initial, mobility, labels, electrode, rates):
    _, height, depth = initial.shape
    plane = (height, depth)
    place = lax.axis_index("space")
    odd = place % 2
    leading = lax.axis_index("tm") == 0
    who = jnp.stack([odd, leading.astype(jnp.int32), place, jnp.int32(lax.axis_size("space"))]).astype(jnp.int32)
    inside = lambda reach: (
        (2 * place + jnp.arange(-reach, 2 + reach) >= 0)
        & (2 * place + jnp.arange(-reach, 2 + reach) < 2 * lax.axis_size("space"))
    ).astype(jnp.float32)

    there = pl.BlockSpec(memory_space=pltpu.HBM)
    fields = (source, initial, mobility, labels, electrode)
    far, near, fixed = pl.pallas_call(
        parcel_kernel,
        out_shape=[jax.ShapeDtypeStruct((n,) + plane, jnp.float32) for n in (PARCEL, PARCEL, OWN)],
        in_specs=[SMEM] + [there] * len(fields),
        out_specs=[VMEM] * 3,
        scratch_shapes=[pltpu.VMEM(v.shape, v.dtype) for v in fields] + [pltpu.SemaphoreType.DMA((len(fields),))],
        name="parcel",
        compiler_params=pltpu.CompilerParams(vmem_limit_bytes=60 << 20),
    )(rates, *fields)
    far, near = traded(far, near)
    static = (who, fixed, far, near)
    tall = (height + 2 * EDGE, depth)

    coarse = (height // 2, depth)
    to_far, to_near, closing = call(
        first_kernel,
        "first",
        static,
        [(17,) + plane] * 2 + [initial.shape],
        windows(height, depth) + [pltpu.VMEM((STEPS, 12) + tall, jnp.float32)] * 2
        + [pltpu.VMEM((6,) + coarse, jnp.float32)],
    )
    got_far, got_near = traded(to_far, to_near)
    opening = arrived(closing, 1)
    states = (to_far, got_far, got_near)

    base, closing, both, rhs, rough_w = call(
        residual_kernel,
        "residual",
        static + states + (opening,),
        [(4,) + coarse] * 2 + [(2, 4) + coarse, (2,) + coarse, (10,) + coarse],
        windows(height, depth)
        + [pltpu.VMEM((STEPS, 12) + tall, jnp.float32), pltpu.VMEM((8,) + plane, jnp.float32)],
    )
    one = arrived(base, 1)
    two = arrived(both, 2)
    three = arrived(closing, 3)
    rhs1 = one + two[1]
    rhs2 = two[0] + three
    pair = jnp.stack([rhs, inner(rhs1, 0, 1)])
    pair = pair + Coupling(inner(rough_w, 0, 3), inside(1)).step(jnp.stack([rhs1, rhs2]))

    flat = lambda v: v.reshape((-1,) + plane)
    unflat = lambda v: v.reshape((-1,) + coarse)
    cargo = lambda c, o: jnp.concatenate([flat(pair), flat(c), o], axis=0)
    to_low = cargo(rough_w[8:10], opening[: SLAB - 1])
    to_high = cargo(rough_w[0:2], opening[1:])
    side_far, side_near = traded(*by_side(odd == 1, to_low, to_high))
    low, high = by_side(odd == 1, unflat(side_far[:3]), unflat(side_near[:3]))
    pair_of = lambda b: b[:4].reshape(pair.shape)
    rough_far = jnp.concatenate([low[4:], rough_w, high[4:]], axis=0)
    pair = jnp.concatenate([pair_of(low), pair, pair_of(high)], axis=1)
    joined = lambda *parts: jnp.concatenate(parts, axis=1)
    count = lax.axis_size("space")
    gap = jnp.zeros_like(pair[:, :2])
    got = sent(pair, 2, [i if i in (0, count - 1) else i + 1 if i % 2 else i - 1 for i in range(count)])
    got = jnp.where(place == 0, joined(gap, got[:, :4]), got)
    got = jnp.where(place == count - 1, joined(got[:, 2:], gap), got)
    mate = sent(got, 0, [i ^ 1 for i in range(count)])
    older = jnp.where(odd == 1, joined(mate[:, 2:], got), joined(got, mate[:, :4]))
    coupling = Coupling(rough_far, inside(6))
    pair = pair + coupling.steps(older, 2)
    got = joined(sent(pair, 4, [i - 2 if i % 2 else i + 2 for i in range(count)]), sent(pair[:, 2:4], 4, range(count)))
    mate = sent(got, 0, [i ^ 1 for i in range(count)])
    centre, beside = got[:, 6:], mate[:, 6:]
    older = jnp.where(
        odd == 1,
        joined(mate[:, 2:6], beside, centre, got[:, :6]),
        joined(got[:, :6], centre, beside, mate[:, :4]),
    )
    correction = pair + coupling.steps(older, 4)

    (density,) = call(
        last_kernel,
        "last",
        static + states + (opening, side_far, side_near, correction),
        [source.shape],
        windows(height, depth)
        + [pltpu.VMEM((STEPS, 12) + tall, jnp.float32)] * 2
        + [pltpu.VMEM((10,) + plane, jnp.float32)],
    )
    return density


def solution(mesh):
    cells = P("space", None, None)
    times = P("tm", "space", None, None)
    return jax.shard_map(
        on_device,
        mesh=mesh,
        in_specs=(times, cells, cells, cells, cells, P()),
        out_specs=times,
        check_vma=False,
    )
```

```python
import jax
import jax.numpy as jnp
from jax import lax
from jax.experimental import pallas as pl
from jax.experimental.pallas import tpu as pltpu
from jax.sharding import PartitionSpec as P

PASSES = 4
DAMPING = 0.8
LATERAL = 0.06
AXIAL = 0.12
STEPS = 4
SLAB = 4
EDGE = 8

VMEM = pl.BlockSpec(memory_space=pltpu.VMEM)
SMEM = pl.BlockSpec(memory_space=pltpu.SMEM)

P_INIT, P_MOB, P_FREE, P_KAP, PARCEL = 12, 16, 20, 24, 27
O_INIT, O_MOB, O_FREE, O_KAP, OWN = 16, 20, 24, 28, 32


def shifted(values, by, axis):
    size = values.shape[axis]
    return pltpu.roll(values, by % size, axis)


def parcel_kernel(rates, source, initial, mobility, labels, electrode, far, near, own):
    odd = lax.rem(lax.axis_index("space"), 2)

    @pl.loop(0, SLAB)
    def _(p):
        kind = labels[p]
        value = jnp.zeros(kind.shape, jnp.float32)
        for n in range(rates.shape[0]):
            value = jnp.where(kind == n, rates[n], value)
        own[O_KAP + p] = value
        open_cell = 1.0 - electrode[p].astype(jnp.float32)
        own[O_FREE + p] = open_cell
        own[O_INIT + p] = initial[p]
        own[O_MOB + p] = mobility[p]
        for t in range(STEPS):
            own[SLAB * t + p] = 0.5 * source[t, p]
        for out in (far, near):
            out[P_INIT + p] = initial[p]
            out[P_MOB + p] = mobility[p]
            out[P_FREE + p] = open_cell

    for out, begin in ((far, odd), (near, 1 - odd)):

        @pl.loop(0, SLAB - 1)
        def _(j):
            out[P_KAP + j] = own[O_KAP + begin + j]
            for t in range(STEPS):
                out[3 * t + j] = own[SLAB * t + begin + j]


def load_static(odd, fixed, far, near, force, begin, mob, kap, open_cell):
    rows = pl.ds(EDGE, fixed.shape[1])

    @pl.loop(0, SLAB)
    def _(p):
        begin[4 + p] = fixed[O_INIT + p]
        mob[4 + p, rows] = fixed[O_MOB + p]
        open_cell[4 + p] = fixed[O_FREE + p]
        kap[3 + p] = fixed[O_KAP + p]
        for t in range(STEPS):
            force[t, 3 + p] = fixed[SLAB * t + p]
        for block, wide in ((far, 8 * odd), (near, 8 - 8 * odd)):
            begin[wide + p] = block[P_INIT + p]
            mob[wide + p, rows] = block[P_MOB + p]
            open_cell[wide + p] = block[P_FREE + p]

    @pl.loop(0, SLAB - 1)
    def _(p):
        for block, wide in ((far, 7 * odd), (near, 7 - 7 * odd)):
            kap[wide + p] = block[P_KAP + p]
            for t in range(STEPS):
                force[t, wide + p] = block[3 * t + p]

    zero = jnp.zeros((EDGE, mob.shape[2]), jnp.float32)

    @pl.loop(0, mob.shape[0])
    def _(p):
        mob[p, pl.ds(0, EDGE)] = zero
        mob[p, pl.ds(mob.shape[1] - EDGE, EDGE)] = zero


def make_weights(mob, weights, first, last):
    height = mob.shape[1] - 2 * EDGE

    @pl.loop(first, last)
    def _(j):
        for r in range(0, height, 8):
            at = lambda p, d: mob[p, pl.ds(EDGE + r + d, 8)]
            here = at(j + 1, 0)
            lane = lax.broadcasted_iota(jnp.int32, here.shape, 1)
            lowest, highest = lane == 0, lane == here.shape[1] - 1
            xl = 0.5 * (here + at(j, 0))
            xh = 0.5 * (here + at(j + 2, 0))
            yl = 0.5 * (here + at(j + 1, -1))
            yh = 0.5 * (here + at(j + 1, 1))
            zl = 0.5 * (here + jnp.where(lowest, 0.0, shifted(here, 1, 1)))
            zh = 0.5 * (here + jnp.where(highest, 0.0, shifted(here, -1, 1)))
            rows = pl.ds(r, 8)
            weights[j, 0, rows] = xl
            weights[j, 1, rows] = xh
            weights[j, 2, rows] = yl
            weights[j, 3, rows] = yh
            weights[j, 4, rows] = jnp.where(lowest, 0.0, 1.5 * zl)
            weights[j, 5, rows] = jnp.where(highest, 0.0, zh)
            weights[j, 6, rows] = 1.0 + (xl + xh + yl + yh + zl + zh) + 0.5 * zh


def clear_edges(cells):
    zero = jnp.zeros((EDGE, cells.shape[-1]), jnp.float32)

    @pl.loop(0, cells.shape[1])
    def _(p):
        for t in range(STEPS):
            cells[t, p, pl.ds(0, EDGE)] = zero
            cells[t, p, pl.ds(cells.shape[2] - EDGE, EDGE)] = zero


def gathered(w, cells, t, p, r):
    here = cells[t, p, pl.ds(EDGE + r, 8)]
    total = w[0] * cells[t, p - 1, pl.ds(EDGE + r, 8)]
    total += w[1] * cells[t, p + 1, pl.ds(EDGE + r, 8)]
    total += w[2] * cells[t, p, pl.ds(EDGE + r - 1, 8)]
    total += w[3] * cells[t, p, pl.ds(EDGE + r + 1, 8)]
    total += w[4] * shifted(here, 1, 1)
    total += w[5] * shifted(here, -1, 1)
    return here, total


def run_sweep(cells, other, weights, kap, open_cell, force, opening, done=0):
    height = cells.shape[2] - 2 * EDGE
    for number in range(done, PASSES):
        source, target = (cells, other) if number % 2 == 0 else (other, cells)

        @pl.loop(number, 10 - number)
        def _(j):
            for r in range(0, height, 8):
                rows = pl.ds(r, 8)
                w = [weights[j, n, rows] for n in range(7)]
                rate = kap[j, rows]
                gain = DAMPING * open_cell[j + 1, rows]
                former = opening[j, rows]
                for t in range(STEPS):
                    here, total = gathered(w, source, t, j + 1, r)
                    pull = rate * jnp.abs(here)
                    residue = force[t, j, rows] + former + total - here * (w[6] + 0.5 * pull)
                    target[t, j + 1, pl.ds(EDGE + r, 8)] = here + gain * residue / (w[6] + pull)
                    former = here


def first_pass(cells, other, weights, kap, open_cell, force):
    height = cells.shape[2] - 2 * EDGE

    @pl.loop(0, 10)
    def _(j):
        for r in range(0, height, 8):
            rows = pl.ds(r, 8)
            w = [weights[j, n, rows] for n in range(7)]
            here, total = gathered(w, cells, 0, j + 1, r)
            pull = kap[j, rows] * jnp.abs(here)
            shared = here + total - here * (w[6] + 0.5 * pull)
            gain = DAMPING * open_cell[j + 1, rows] / (w[6] + pull)
            for t in range(STEPS):
                other[t, j + 1, pl.ds(EDGE + r, 8)] = here + gain * (force[t, j, rows] + shared)


def halved(read):
    return 0.25 * ((read(0, 0) + read(0, 1)) + (read(1, 0) + read(1, 1)))


def first_kernel(who, fixed, far, near, to_far, to_near, closing,
                 force, begin, mob, kap, open_cell, weights, cells, other, rough):
    odd = who[0]
    height = fixed.shape[1]
    load_static(odd, fixed, far, near, force, begin, mob, kap, open_cell)
    make_weights(mob, weights, 0, 10)
    clear_edges(cells)

    @pl.loop(0, 12)
    def _(p):
        cells[0, p, pl.ds(EDGE, height)] = begin[p]

    clear_edges(other)
    first_pass(cells, other, weights, kap, open_cell, force)
    run_sweep(cells, other, weights, kap, open_cell, force, begin.at[pl.ds(1, 10)], 1)
    for p in range(SLAB):
        closing[p] = cells[STEPS - 1, 4 + p, pl.ds(EDGE, height)]
    half = height // 2
    for a in range(6):
        rough[a] = halved(lambda x, y: mob[2 * a + x, pl.ds(EDGE + y, half, stride=2)])
    for out, base in ((to_far, 4 - 4 * odd), (to_near, 4 * odd)):
        for t in range(STEPS):
            for p in range(SLAB):
                out[4 * t + p] = cells[t, 4 + p, pl.ds(EDGE, height)]
        out[16, pl.ds(0, half)] = rough[base]
        out[16, pl.ds(half, half)] = rough[base + 1]


def residual_kernel(who, fixed, far, near, own, low_far, low_near, arriving,
                    base, closing, both, rhs, rough, force, begin, mob, kap, open_cell, weights, cells, residues):
    odd, leading, place, count = who[0], who[1], who[2], who[3]
    height = fixed.shape[1]
    half = height // 2
    load_static(odd, fixed, far, near, force, begin, mob, kap, open_cell)
    make_weights(mob, weights, 1, 9)
    clear_edges(cells)
    rows = pl.ds(EDGE, height)
    for t in range(STEPS):

        @pl.loop(0, SLAB)
        def _(p):
            cells[t, 4 + p, rows] = own[4 * t + p]
            cells[t, 8 * odd + p, rows] = low_far[4 * t + p]
            cells[t, 8 - 8 * odd + p, rows] = low_near[4 * t + p]

    @pl.loop(1, 9)
    def _(j):
        for r in range(0, height, 8):
            rows = pl.ds(r, 8)
            w = [weights[j, n, rows] for n in range(7)]
            rate = kap[j, rows]
            former = jnp.where(leading == 1, begin[j + 1, rows], 0.0)
            acc = jnp.zeros_like(former)
            for t in range(STEPS):
                here, total = gathered(w, cells, t, j + 1, r)
                pull = rate * jnp.abs(here)
                acc += force[t, j, rows] + former + total - here * (w[6] + 0.5 * pull)
                former = here
            residues[j - 1, rows] = acc

    for a in range(4):
        coarse = 2 * place - 1 + a
        inside = jnp.logical_and(coarse >= 0, coarse < 2 * count)
        value = halved(lambda x, y: residues[2 * a + x, pl.ds(y, half, stride=2)])
        base[a] = jnp.where(inside, value, 0.0)
        closing[a] = halved(lambda x, y: cells[STEPS - 1, 2 + 2 * a + x, pl.ds(EDGE + y, half, stride=2)])
        both[0, a] = base[a]
        both[1, a] = closing[a]
    for a in range(2):
        rhs[a] = base[1 + a] + halved(lambda x, y: arriving[2 * a + x, pl.ds(y, half, stride=2)])
        for block, at in ((low_far, 8 * odd), (low_near, 8 - 8 * odd)):
            rough[at + a] = block[16, pl.ds(half * a, half)]
    for a in range(6):
        rough[2 + a] = halved(lambda x, y: mob[2 * a + x, pl.ds(EDGE + y, half, stride=2)])


def join_kernel(who, side_far, side_near, pair, rough, arriving, pairs, roughs, opening):
    odd = who[0]
    half = pair.shape[2]
    for a in range(2):
        for q in range(2):
            pairs[q, 2 + a] = pair[q, a]
    for a in range(10):
        roughs[2 + a] = rough[a]
    for p in range(SLAB):
        opening[3 + p] = arriving[p]
    for block, up in ((side_far, odd), (side_near, 1 - odd)):
        for a in range(2):
            rows = pl.ds(half * a, half)
            for q in range(2):
                pairs[q, 4 * up + a] = block[q, rows]
            roughs[12 * up + a] = block[2, rows]
        for j in range(SLAB - 1):
            opening[7 * up + j] = block[3 + j]


def last_kernel(who, fixed, far, near, own, low_far, low_near, arriving, correction,
                out, force, begin, mob, kap, open_cell, weights, cells, other, opening):
    odd, leading = who[0], who[1]
    height = fixed.shape[1]
    half = height // 2
    load_static(odd, fixed, far, near, force, begin, mob, kap, open_cell)
    make_weights(mob, weights, 0, 10)
    clear_edges(cells)
    for y in range(2):
        rows = pl.ds(y, half, stride=2)
        into = pl.ds(EDGE + y, half, stride=2)

        @pl.loop(0, SLAB)
        def _(p):
            for block, at in ((own, 4), (low_far, 8 * odd), (low_near, 8 - 8 * odd)):
                plane = at + p
                change = open_cell[plane, rows] * correction[0, plane // 2]
                for t in range(STEPS):
                    cells[t, plane, into] = block[4 * t + p, rows] + change

        @pl.loop(0, 10)
        def _(j):
            base = jnp.where(leading == 1, begin[j + 1, rows], arriving[j, rows])
            opening[j, rows] = base + open_cell[j + 1, rows] * correction[1, (j + 1) // 2]

    clear_edges(other)
    run_sweep(cells, other, weights, kap, open_cell, force, opening)
    for t in range(STEPS):
        for p in range(SLAB):
            out[t, p] = cells[t, 4 + p, pl.ds(EDGE, height)]


def windows(height, depth):
    plane = (height, depth)
    tall = (height + 2 * EDGE, depth)
    f32 = jnp.float32
    return [
        pltpu.VMEM((STEPS, 10) + plane, f32),
        pltpu.VMEM((12,) + plane, f32),
        pltpu.VMEM((12,) + tall, f32),
        pltpu.VMEM((10,) + plane, f32),
        pltpu.VMEM((12,) + plane, f32),
        pltpu.VMEM((10, 7) + plane, f32),
    ]


def call(kernel, name, inputs, outputs, scratch, grant=28):
    return pl.pallas_call(
        kernel,
        out_shape=[jax.ShapeDtypeStruct(o, jnp.float32) for o in outputs],
        in_specs=[SMEM] + [VMEM] * (len(inputs) - 1),
        out_specs=[VMEM] * len(outputs),
        scratch_shapes=scratch,
        name=name,
        compiler_params=pltpu.CompilerParams(vmem_limit_bytes=grant << 20),
    )(*inputs)


def inner(values, dim, cut):
    return lax.slice_in_dim(values, cut, values.shape[dim] - cut, axis=dim)


class Coupling:
    def __init__(self, mob, inside):
        centre = mob[1:-1]
        padded = jnp.pad(centre, ((0, 0), (1, 1), (1, 1)))
        keep = inside[1:-1, None, None]
        half = 0.5 * LATERAL * keep
        axial = 0.5 * AXIAL * keep
        self.xl = half * (centre + mob[:-2])
        self.xh = half * (centre + mob[2:])
        self.yl = half * (centre + padded[:, :-2, 1:-1])
        self.yh = half * (centre + padded[:, 2:, 1:-1])
        self.zl = axial * (centre + padded[:, 1:-1, :-2])
        self.zh = axial * (centre + padded[:, 1:-1, 2:])
        self.own = keep - (self.xl + self.xh + self.yl + self.yh + self.zl + self.zh)

    def step(self, values):
        planes = values.shape[-3] - 2
        cut = (self.own.shape[0] - planes) // 2
        take = lambda w: inner(w, 0, cut)
        centre = values[..., 1:-1, :, :]
        pads = [(0, 0)] * (values.ndim - 2) + [(1, 1), (1, 1)]
        padded = jnp.pad(centre, pads)
        return (
            take(self.own) * centre
            + take(self.xl) * values[..., :-2, :, :]
            + take(self.xh) * values[..., 2:, :, :]
            + take(self.yl) * padded[..., :-2, 1:-1]
            + take(self.yh) * padded[..., 2:, 1:-1]
            + take(self.zl) * padded[..., 1:-1, :-2]
            + take(self.zh) * padded[..., 1:-1, 2:]
        )

    def steps(self, values, count):
        for number in range(count):
            values = self.step(values)
        return values


def sent(value, steps, to):
    times = lax.axis_size("tm")
    count = lax.axis_size("space")
    pairs = [
        (k * count + i, (k + steps) * count + to[i])
        for k in range(times - steps)
        for i in range(count)
        if 0 <= to[i] < count
    ]
    return lax.ppermute(value, ("tm", "space"), pairs)


def traded(far, near):
    count = lax.axis_size("space")
    far_of = [i + 1 if i % 2 else i - 1 for i in range(count)]
    return sent(far, 0, far_of), sent(near, 0, [i ^ 1 for i in range(count)])


def by_side(odd, far, near):
    return jnp.where(odd, near, far), jnp.where(odd, far, near)


def arrived(value, steps):
    times = lax.axis_size("tm")
    return lax.ppermute(value, "tm", [(k, k + steps) for k in range(times - steps)])


def on_device(source, initial, mobility, labels, electrode, rates):
    _, height, depth = initial.shape
    plane = (height, depth)
    place = lax.axis_index("space")
    odd = place % 2
    leading = lax.axis_index("tm") == 0
    who = jnp.stack([odd, leading.astype(jnp.int32), place, jnp.int32(lax.axis_size("space"))]).astype(jnp.int32)
    inside = lambda reach: (
        (2 * place + jnp.arange(-reach, 2 + reach) >= 0)
        & (2 * place + jnp.arange(-reach, 2 + reach) < 2 * lax.axis_size("space"))
    ).astype(jnp.float32)

    fields = (source, initial, mobility, labels, electrode)
    far, near, fixed = pl.pallas_call(
        parcel_kernel,
        out_shape=[jax.ShapeDtypeStruct((n,) + plane, jnp.float32) for n in (PARCEL, PARCEL, OWN)],
        in_specs=[SMEM] + [VMEM] * len(fields),
        out_specs=[VMEM] * 3,
        name="parcel",
        compiler_params=pltpu.CompilerParams(vmem_limit_bytes=60 << 20),
    )(rates, *fields)
    far, near = traded(far, near)
    static = (who, fixed, far, near)
    tall = (height + 2 * EDGE, depth)

    coarse = (height // 2, depth)
    to_far, to_near, closing = call(
        first_kernel,
        "first",
        static,
        [(17,) + plane] * 2 + [initial.shape],
        windows(height, depth) + [pltpu.VMEM((STEPS, 12) + tall, jnp.float32)] * 2
        + [pltpu.VMEM((6,) + coarse, jnp.float32)],
    )
    got_far, got_near = traded(to_far, to_near)
    opening = arrived(closing, 1)
    states = (to_far, got_far, got_near)

    base, closing, both, rhs, rough_w = call(
        residual_kernel,
        "residual",
        static + states + (opening,),
        [(4,) + coarse] * 2 + [(2, 4) + coarse, (2,) + coarse, (10,) + coarse],
        windows(height, depth)
        + [pltpu.VMEM((STEPS, 12) + tall, jnp.float32), pltpu.VMEM((8,) + plane, jnp.float32)],
    )
    one = arrived(base, 1)
    two = arrived(both, 2)
    three = arrived(closing, 3)
    rhs1 = one + two[1]
    rhs2 = two[0] + three
    pair = jnp.stack([rhs, inner(rhs1, 0, 1)])
    pair = pair + Coupling(inner(rough_w, 0, 3), inside(1)).step(jnp.stack([rhs1, rhs2]))

    flat = lambda v: v.reshape((-1,) + plane)
    cargo = lambda c, o: jnp.concatenate([flat(pair), flat(c), o], axis=0)
    to_low = cargo(rough_w[8:10], opening[: SLAB - 1])
    to_high = cargo(rough_w[0:2], opening[1:])
    side_far, side_near = traded(*by_side(odd == 1, to_low, to_high))
    pair, rough_far, opening = call(
        join_kernel,
        "join",
        (who, side_far, side_near, pair, rough_w, opening),
        [(2, 6) + coarse, (14,) + coarse, (10,) + plane],
        [],
        12,
    )
    joined = lambda *parts: jnp.concatenate(parts, axis=1)
    count = lax.axis_size("space")
    gap = jnp.zeros_like(pair[:, :2])
    got = sent(pair, 2, [i if i in (0, count - 1) else i + 1 if i % 2 else i - 1 for i in range(count)])
    got = jnp.where(place == 0, joined(gap, got[:, :4]), got)
    got = jnp.where(place == count - 1, joined(got[:, 2:], gap), got)
    mate = sent(got, 0, [i ^ 1 for i in range(count)])
    older = jnp.where(odd == 1, joined(mate[:, 2:], got), joined(got, mate[:, :4]))
    coupling = Coupling(rough_far, inside(6))
    pair = pair + coupling.steps(older, 2)
    got = joined(sent(pair, 4, [i - 2 if i % 2 else i + 2 for i in range(count)]), sent(pair[:, 2:4], 4, range(count)))
    mate = sent(got, 0, [i ^ 1 for i in range(count)])
    centre, beside = got[:, 6:], mate[:, 6:]
    older = jnp.where(
        odd == 1,
        joined(mate[:, 2:6], beside, centre, got[:, :6]),
        joined(got[:, :6], centre, beside, mate[:, :4]),
    )
    correction = pair + coupling.steps(older, 4)

    (density,) = call(
        last_kernel,
        "last",
        static + states + (opening, correction),
        [source.shape],
        windows(height, depth)
        + [pltpu.VMEM((STEPS, 12) + tall, jnp.float32)] * 2
        + [pltpu.VMEM((10,) + plane, jnp.float32)],
    )
    return density


def solution(mesh):
    cells = P("space", None, None)
    times = P("tm", "space", None, None)
    return jax.shard_map(
        on_device,
        mesh=mesh,
        in_specs=(times, cells, cells, cells, cells, P()),
        out_specs=times,
        check_vma=False,
    )
```

```python
import jax
import jax.numpy as jnp
from jax import lax
from jax.experimental import pallas as pl
from jax.experimental.pallas import tpu as pltpu
from jax.sharding import PartitionSpec as P

PASSES = 4
DAMPING = 0.8
LATERAL = 0.06
AXIAL = 0.12
STEPS = 4
SLAB = 4
EDGE = 8

VMEM = pl.BlockSpec(memory_space=pltpu.VMEM)
SMEM = pl.BlockSpec(memory_space=pltpu.SMEM)
HBM = pl.BlockSpec(memory_space=pltpu.HBM)

P_INIT, P_MOB, P_FREE, P_KAP, PARCEL = 12, 16, 20, 24, 27
O_INIT, O_MOB, O_FREE, O_KAP, OWN = 16, 20, 24, 28, 32


def shifted(values, by, axis):
    size = values.shape[axis]
    return pltpu.roll(values, by % size, axis)


def parcel_kernel(rates, source, initial, mobility, labels, electrode, far, near, own):
    odd = lax.rem(lax.axis_index("space"), 2)

    @pl.loop(0, SLAB)
    def _(p):
        kind = labels[p]
        value = jnp.zeros(kind.shape, jnp.float32)
        for n in range(rates.shape[0]):
            value = jnp.where(kind == n, rates[n], value)
        own[O_KAP + p] = value
        open_cell = 1.0 - electrode[p].astype(jnp.float32)
        own[O_FREE + p] = open_cell
        own[O_INIT + p] = initial[p]
        own[O_MOB + p] = mobility[p]
        for t in range(STEPS):
            own[SLAB * t + p] = 0.5 * source[t, p]
        for out in (far, near):
            out[P_INIT + p] = initial[p]
            out[P_MOB + p] = mobility[p]
            out[P_FREE + p] = open_cell

    for out, begin in ((far, odd), (near, 1 - odd)):

        @pl.loop(0, SLAB - 1)
        def _(j):
            out[P_KAP + j] = own[O_KAP + begin + j]
            for t in range(STEPS):
                out[3 * t + j] = own[SLAB * t + begin + j]


def start_static(odd, fixed, far, near, force, begin, mob, kap, open_cell, done):
    height = fixed.shape[1]
    zero = jnp.zeros((EDGE, mob.shape[2]), jnp.float32)

    @pl.loop(0, mob.shape[0])
    def _(p):
        mob[p, pl.ds(0, EDGE)] = zero
        mob[p, pl.ds(EDGE + height, EDGE)] = zero

    moves = []
    own_at = (O_INIT, O_MOB, O_FREE, O_KAP)
    side_at = (P_INIT, P_MOB, P_FREE, P_KAP)
    for block, count, (i, m, o, k), deep, shallow in (
        (fixed, SLAB, own_at, 4, 3),
        (far, SLAB - 1, side_at, 8 * odd, 7 * odd),
        (near, SLAB - 1, side_at, 8 - 8 * odd, 7 - 7 * odd),
    ):
        window = pl.ds(deep, SLAB)
        moves.append((block.at[pl.ds(m, SLAB)], mob.at[window, pl.ds(EDGE, height)]))
        moves.append((block.at[pl.ds(i, SLAB)], begin.at[window]))
        moves.append((block.at[pl.ds(o, SLAB)], open_cell.at[window]))
        moves.append((block.at[pl.ds(k, count)], kap.at[pl.ds(shallow, count)]))
        for t in range(STEPS):
            moves.append((block.at[pl.ds(count * t, count)], force.at[t, pl.ds(shallow, count)]))
    copies = [pltpu.make_async_copy(here, there, done.at[n]) for n, (here, there) in enumerate(moves)]
    for copy in copies:
        copy.start()
    return copies


def finish(copies):
    for copy in copies:
        copy.wait()


def make_weights(mob, weights, first, last):
    height = mob.shape[1] - 2 * EDGE

    @pl.loop(first, last)
    def _(j):
        for r in range(0, height, 8):
            at = lambda p, d: mob[p, pl.ds(EDGE + r + d, 8)]
            here = at(j + 1, 0)
            lane = lax.broadcasted_iota(jnp.int32, here.shape, 1)
            lowest, highest = lane == 0, lane == here.shape[1] - 1
            xl = 0.5 * (here + at(j, 0))
            xh = 0.5 * (here + at(j + 2, 0))
            yl = 0.5 * (here + at(j + 1, -1))
            yh = 0.5 * (here + at(j + 1, 1))
            zl = 0.5 * (here + jnp.where(lowest, 0.0, shifted(here, 1, 1)))
            zh = 0.5 * (here + jnp.where(highest, 0.0, shifted(here, -1, 1)))
            rows = pl.ds(r, 8)
            weights[j, 0, rows] = xl
            weights[j, 1, rows] = xh
            weights[j, 2, rows] = yl
            weights[j, 3, rows] = yh
            weights[j, 4, rows] = jnp.where(lowest, 0.0, 1.5 * zl)
            weights[j, 5, rows] = jnp.where(highest, 0.0, zh)
            weights[j, 6, rows] = 1.0 + (xl + xh + yl + yh + zl + zh) + 0.5 * zh


def clear_edges(cells):
    zero = jnp.zeros((EDGE, cells.shape[-1]), jnp.float32)

    @pl.loop(0, cells.shape[1])
    def _(p):
        for t in range(STEPS):
            cells[t, p, pl.ds(0, EDGE)] = zero
            cells[t, p, pl.ds(cells.shape[2] - EDGE, EDGE)] = zero


def gathered(w, cells, t, p, r):
    here = cells[t, p, pl.ds(EDGE + r, 8)]
    total = w[0] * cells[t, p - 1, pl.ds(EDGE + r, 8)]
    total += w[1] * cells[t, p + 1, pl.ds(EDGE + r, 8)]
    total += w[2] * cells[t, p, pl.ds(EDGE + r - 1, 8)]
    total += w[3] * cells[t, p, pl.ds(EDGE + r + 1, 8)]
    total += w[4] * shifted(here, 1, 1)
    total += w[5] * shifted(here, -1, 1)
    return here, total


def run_sweep(cells, other, weights, kap, open_cell, force, opening, done=0):
    height = cells.shape[2] - 2 * EDGE
    for number in range(done, PASSES):
        source, target = (cells, other) if number % 2 == 0 else (other, cells)

        @pl.loop(number, 10 - number)
        def _(j):
            for r in range(0, height, 8):
                rows = pl.ds(r, 8)
                w = [weights[j, n, rows] for n in range(7)]
                rate = kap[j, rows]
                gain = DAMPING * open_cell[j + 1, rows]
                former = opening[j, rows]
                for t in range(STEPS):
                    here, total = gathered(w, source, t, j + 1, r)
                    pull = rate * jnp.abs(here)
                    residue = force[t, j, rows] + former + total - here * (w[6] + 0.5 * pull)
                    target[t, j + 1, pl.ds(EDGE + r, 8)] = here + gain * residue / (w[6] + pull)
                    former = here


def first_pass(cells, other, weights, kap, open_cell, force):
    height = cells.shape[2] - 2 * EDGE

    @pl.loop(0, 10)
    def _(j):
        for r in range(0, height, 8):
            rows = pl.ds(r, 8)
            w = [weights[j, n, rows] for n in range(7)]
            here, total = gathered(w, cells, 0, j + 1, r)
            pull = kap[j, rows] * jnp.abs(here)
            shared = here + total - here * (w[6] + 0.5 * pull)
            gain = DAMPING * open_cell[j + 1, rows] / (w[6] + pull)
            for t in range(STEPS):
                other[t, j + 1, pl.ds(EDGE + r, 8)] = here + gain * (force[t, j, rows] + shared)


def halved(read):
    return 0.25 * ((read(0, 0) + read(0, 1)) + (read(1, 0) + read(1, 1)))


def first_kernel(who, fixed, far, near, to_far, to_near, closing,
                 force, begin, mob, kap, open_cell, weights, cells, other, rough, done):
    odd = who[0]
    height = fixed.shape[1]
    copies = start_static(odd, fixed, far, near, force, begin, mob, kap, open_cell, done)
    clear_edges(cells)
    clear_edges(other)
    finish(copies)
    make_weights(mob, weights, 0, 10)

    @pl.loop(0, 12)
    def _(p):
        cells[0, p, pl.ds(EDGE, height)] = begin[p]

    first_pass(cells, other, weights, kap, open_cell, force)
    run_sweep(cells, other, weights, kap, open_cell, force, begin.at[pl.ds(1, 10)], 1)
    for p in range(SLAB):
        closing[p] = cells[STEPS - 1, 4 + p, pl.ds(EDGE, height)]
    half = height // 2
    for a in range(6):
        rough[a] = halved(lambda x, y: mob[2 * a + x, pl.ds(EDGE + y, half, stride=2)])
    for out, base in ((to_far, 4 - 4 * odd), (to_near, 4 * odd)):
        for t in range(STEPS):
            for p in range(SLAB):
                out[4 * t + p] = cells[t, 4 + p, pl.ds(EDGE, height)]
        out[16, pl.ds(0, half)] = rough[base]
        out[16, pl.ds(half, half)] = rough[base + 1]


def residual_kernel(who, fixed, far, near, own, low_far, low_near, arriving,
                    base, closing, both, rhs, rough, force, begin, mob, kap, open_cell, weights, cells, residues, done):
    odd, leading, place, count = who[0], who[1], who[2], who[3]
    height = fixed.shape[1]
    half = height // 2
    copies = start_static(odd, fixed, far, near, force, begin, mob, kap, open_cell, done)
    clear_edges(cells)
    rows = pl.ds(EDGE, height)
    for t in range(STEPS):

        @pl.loop(0, SLAB)
        def _(p):
            cells[t, 4 + p, rows] = own[4 * t + p]
            cells[t, 8 * odd + p, rows] = low_far[4 * t + p]
            cells[t, 8 - 8 * odd + p, rows] = low_near[4 * t + p]

    finish(copies)
    make_weights(mob, weights, 1, 9)

    @pl.loop(1, 9)
    def _(j):
        for r in range(0, height, 8):
            rows = pl.ds(r, 8)
            w = [weights[j, n, rows] for n in range(7)]
            rate = kap[j, rows]
            former = jnp.where(leading == 1, begin[j + 1, rows], 0.0)
            acc = jnp.zeros_like(former)
            for t in range(STEPS):
                here, total = gathered(w, cells, t, j + 1, r)
                pull = rate * jnp.abs(here)
                acc += force[t, j, rows] + former + total - here * (w[6] + 0.5 * pull)
                former = here
            residues[j - 1, rows] = acc

    for a in range(4):
        coarse = 2 * place - 1 + a
        inside = jnp.logical_and(coarse >= 0, coarse < 2 * count)
        value = halved(lambda x, y: residues[2 * a + x, pl.ds(y, half, stride=2)])
        base[a] = jnp.where(inside, value, 0.0)
        closing[a] = halved(lambda x, y: cells[STEPS - 1, 2 + 2 * a + x, pl.ds(EDGE + y, half, stride=2)])
        both[0, a] = base[a]
        both[1, a] = closing[a]
    for a in range(2):
        rhs[a] = base[1 + a] + halved(lambda x, y: arriving[2 * a + x, pl.ds(y, half, stride=2)])
        for block, at in ((low_far, 8 * odd), (low_near, 8 - 8 * odd)):
            rough[at + a] = block[16, pl.ds(half * a, half)]
    for a in range(6):
        rough[2 + a] = halved(lambda x, y: mob[2 * a + x, pl.ds(EDGE + y, half, stride=2)])


def join_kernel(who, side_far, side_near, pair, rough, arriving, pairs, roughs, opening):
    odd = who[0]
    half = pair.shape[2]
    for a in range(2):
        for q in range(2):
            pairs[q, 2 + a] = pair[q, a]
    for a in range(10):
        roughs[2 + a] = rough[a]
    for p in range(SLAB):
        opening[3 + p] = arriving[p]
    for block, up in ((side_far, odd), (side_near, 1 - odd)):
        for a in range(2):
            rows = pl.ds(half * a, half)
            for q in range(2):
                pairs[q, 4 * up + a] = block[q, rows]
            roughs[12 * up + a] = block[2, rows]
        for j in range(SLAB - 1):
            opening[7 * up + j] = block[3 + j]


def last_kernel(who, fixed, far, near, own, low_far, low_near, arriving, correction,
                out, force, begin, mob, kap, open_cell, weights, cells, other, opening, done):
    odd, leading = who[0], who[1]
    height = fixed.shape[1]
    half = height // 2
    copies = start_static(odd, fixed, far, near, force, begin, mob, kap, open_cell, done)
    clear_edges(cells)
    clear_edges(other)
    finish(copies)
    make_weights(mob, weights, 0, 10)
    for y in range(2):
        rows = pl.ds(y, half, stride=2)
        into = pl.ds(EDGE + y, half, stride=2)

        @pl.loop(0, SLAB)
        def _(p):
            for block, at in ((own, 4), (low_far, 8 * odd), (low_near, 8 - 8 * odd)):
                plane = at + p
                change = open_cell[plane, rows] * correction[0, plane // 2]
                for t in range(STEPS):
                    cells[t, plane, into] = block[4 * t + p, rows] + change

        @pl.loop(0, 10)
        def _(j):
            base = jnp.where(leading == 1, begin[j + 1, rows], arriving[j, rows])
            opening[j, rows] = base + open_cell[j + 1, rows] * correction[1, (j + 1) // 2]

    run_sweep(cells, other, weights, kap, open_cell, force, opening)
    for t in range(STEPS):
        for p in range(SLAB):
            out[t, p] = cells[t, 4 + p, pl.ds(EDGE, height)]


def windows(height, depth):
    plane = (height, depth)
    tall = (height + 2 * EDGE, depth)
    f32 = jnp.float32
    return [
        pltpu.VMEM((STEPS, 10) + plane, f32),
        pltpu.VMEM((12,) + plane, f32),
        pltpu.VMEM((12,) + tall, f32),
        pltpu.VMEM((10,) + plane, f32),
        pltpu.VMEM((12,) + plane, f32),
        pltpu.VMEM((10, 7) + plane, f32),
    ]


def call(kernel, name, inputs, outputs, scratch, grant=24, held=3):
    return pl.pallas_call(
        kernel,
        out_shape=[jax.ShapeDtypeStruct(o, jnp.float32) for o in outputs],
        in_specs=[SMEM] + [HBM] * held + [VMEM] * (len(inputs) - 1 - held),
        out_specs=[VMEM] * len(outputs),
        scratch_shapes=scratch + [pltpu.SemaphoreType.DMA((24,))] * (held > 0),
        name=name,
        compiler_params=pltpu.CompilerParams(vmem_limit_bytes=grant << 20),
    )(*inputs)


def inner(values, dim, cut):
    return lax.slice_in_dim(values, cut, values.shape[dim] - cut, axis=dim)


class Coupling:
    def __init__(self, mob, inside):
        centre = mob[1:-1]
        padded = jnp.pad(centre, ((0, 0), (1, 1), (1, 1)))
        keep = inside[1:-1, None, None]
        half = 0.5 * LATERAL * keep
        axial = 0.5 * AXIAL * keep
        self.xl = half * (centre + mob[:-2])
        self.xh = half * (centre + mob[2:])
        self.yl = half * (centre + padded[:, :-2, 1:-1])
        self.yh = half * (centre + padded[:, 2:, 1:-1])
        self.zl = axial * (centre + padded[:, 1:-1, :-2])
        self.zh = axial * (centre + padded[:, 1:-1, 2:])
        self.own = keep - (self.xl + self.xh + self.yl + self.yh + self.zl + self.zh)

    def step(self, values):
        planes = values.shape[-3] - 2
        cut = (self.own.shape[0] - planes) // 2
        take = lambda w: inner(w, 0, cut)
        centre = values[..., 1:-1, :, :]
        pads = [(0, 0)] * (values.ndim - 2) + [(1, 1), (1, 1)]
        padded = jnp.pad(centre, pads)
        return (
            take(self.own) * centre
            + take(self.xl) * values[..., :-2, :, :]
            + take(self.xh) * values[..., 2:, :, :]
            + take(self.yl) * padded[..., :-2, 1:-1]
            + take(self.yh) * padded[..., 2:, 1:-1]
            + take(self.zl) * padded[..., 1:-1, :-2]
            + take(self.zh) * padded[..., 1:-1, 2:]
        )

    def steps(self, values, count):
        for number in range(count):
            values = self.step(values)
        return values


def sent(value, steps, to):
    times = lax.axis_size("tm")
    count = lax.axis_size("space")
    pairs = [
        (k * count + i, (k + steps) * count + to[i])
        for k in range(times - steps)
        for i in range(count)
        if 0 <= to[i] < count
    ]
    return lax.ppermute(value, ("tm", "space"), pairs)


def traded(far, near):
    count = lax.axis_size("space")
    far_of = [i + 1 if i % 2 else i - 1 for i in range(count)]
    return sent(far, 0, far_of), sent(near, 0, [i ^ 1 for i in range(count)])


def by_side(odd, far, near):
    return jnp.where(odd, near, far), jnp.where(odd, far, near)


def arrived(value, steps):
    times = lax.axis_size("tm")
    return lax.ppermute(value, "tm", [(k, k + steps) for k in range(times - steps)])


def on_device(source, initial, mobility, labels, electrode, rates):
    _, height, depth = initial.shape
    plane = (height, depth)
    place = lax.axis_index("space")
    odd = place % 2
    leading = lax.axis_index("tm") == 0
    who = jnp.stack([odd, leading.astype(jnp.int32), place, jnp.int32(lax.axis_size("space"))]).astype(jnp.int32)
    inside = lambda reach: (
        (2 * place + jnp.arange(-reach, 2 + reach) >= 0)
        & (2 * place + jnp.arange(-reach, 2 + reach) < 2 * lax.axis_size("space"))
    ).astype(jnp.float32)

    fields = (source, initial, mobility, labels, electrode)
    far, near, fixed = pl.pallas_call(
        parcel_kernel,
        out_shape=[jax.ShapeDtypeStruct((n,) + plane, jnp.float32) for n in (PARCEL, PARCEL, OWN)],
        in_specs=[SMEM] + [VMEM] * len(fields),
        out_specs=[VMEM] * 3,
        name="parcel",
        compiler_params=pltpu.CompilerParams(vmem_limit_bytes=60 << 20),
    )(rates, *fields)
    far, near = traded(far, near)
    fixed, far, near = (pltpu.with_memory_space_constraint(v, pltpu.HBM) for v in (fixed, far, near))
    static = (who, fixed, far, near)
    tall = (height + 2 * EDGE, depth)

    coarse = (height // 2, depth)
    to_far, to_near, closing = call(
        first_kernel,
        "first",
        static,
        [(17,) + plane] * 2 + [initial.shape],
        windows(height, depth) + [pltpu.VMEM((STEPS, 12) + tall, jnp.float32)] * 2
        + [pltpu.VMEM((6,) + coarse, jnp.float32)],
    )
    got_far, got_near = traded(to_far, to_near)
    opening = arrived(closing, 1)
    states = (to_far, got_far, got_near)

    base, closing, both, rhs, rough_w = call(
        residual_kernel,
        "residual",
        static + states + (opening,),
        [(4,) + coarse] * 2 + [(2, 4) + coarse, (2,) + coarse, (10,) + coarse],
        windows(height, depth)
        + [pltpu.VMEM((STEPS, 12) + tall, jnp.float32), pltpu.VMEM((8,) + plane, jnp.float32)],
    )
    one = arrived(base, 1)
    two = arrived(both, 2)
    three = arrived(closing, 3)
    rhs1 = one + two[1]
    rhs2 = two[0] + three
    pair = jnp.stack([rhs, inner(rhs1, 0, 1)])
    pair = pair + Coupling(inner(rough_w, 0, 3), inside(1)).step(jnp.stack([rhs1, rhs2]))

    flat = lambda v: v.reshape((-1,) + plane)
    cargo = lambda c, o: jnp.concatenate([flat(pair), flat(c), o], axis=0)
    to_low = cargo(rough_w[8:10], opening[: SLAB - 1])
    to_high = cargo(rough_w[0:2], opening[1:])
    side_far, side_near = traded(*by_side(odd == 1, to_low, to_high))
    pair, rough_far, opening = call(
        join_kernel,
        "join",
        (who, side_far, side_near, pair, rough_w, opening),
        [(2, 6) + coarse, (14,) + coarse, (10,) + plane],
        [],
        12,
        0,
    )
    joined = lambda *parts: jnp.concatenate(parts, axis=1)
    count = lax.axis_size("space")
    gap = jnp.zeros_like(pair[:, :2])
    got = sent(pair, 2, [i if i in (0, count - 1) else i + 1 if i % 2 else i - 1 for i in range(count)])
    got = jnp.where(place == 0, joined(gap, got[:, :4]), got)
    got = jnp.where(place == count - 1, joined(got[:, 2:], gap), got)
    mate = sent(got, 0, [i ^ 1 for i in range(count)])
    older = jnp.where(odd == 1, joined(mate[:, 2:], got), joined(got, mate[:, :4]))
    coupling = Coupling(rough_far, inside(6))
    pair = pair + coupling.steps(older, 2)
    got = joined(sent(pair, 4, [i - 2 if i % 2 else i + 2 for i in range(count)]), sent(pair[:, 2:4], 4, range(count)))
    mate = sent(got, 0, [i ^ 1 for i in range(count)])
    centre, beside = got[:, 6:], mate[:, 6:]
    older = jnp.where(
        odd == 1,
        joined(mate[:, 2:6], beside, centre, got[:, :6]),
        joined(got[:, :6], centre, beside, mate[:, :4]),
    )
    correction = pair + coupling.steps(older, 4)

    (density,) = call(
        last_kernel,
        "last",
        static + states + (opening, correction),
        [source.shape],
        windows(height, depth)
        + [pltpu.VMEM((STEPS, 12) + tall, jnp.float32)] * 2
        + [pltpu.VMEM((10,) + plane, jnp.float32)],
    )
    return density


def solution(mesh):
    cells = P("space", None, None)
    times = P("tm", "space", None, None)
    return jax.shard_map(
        on_device,
        mesh=mesh,
        in_specs=(times, cells, cells, cells, cells, P()),
        out_specs=times,
        check_vma=False,
    )
```

```python
import jax
import jax.numpy as jnp
from jax import lax
from jax.experimental import pallas as pl
from jax.experimental.pallas import tpu as pltpu
from jax.sharding import PartitionSpec as P

PASSES = 4
DAMPING = 0.8
LATERAL = 0.06
AXIAL = 0.12
STEPS = 4
SLAB = 4
EDGE = 8

VMEM = pl.BlockSpec(memory_space=pltpu.VMEM)
SMEM = pl.BlockSpec(memory_space=pltpu.SMEM)
HBM = pl.BlockSpec(memory_space=pltpu.HBM)
ANY = pl.BlockSpec(memory_space=pl.ANY)

P_INIT, P_MOB, P_FREE, P_KAP, PARCEL = 12, 16, 20, 24, 27
O_INIT, O_MOB, O_FREE, O_KAP, OWN = 16, 20, 24, 28, 32


def shifted(values, by, axis):
    size = values.shape[axis]
    return pltpu.roll(values, by % size, axis)


def parcel_kernel(rates, source, initial, mobility, labels, electrode, far, near, own):
    odd = lax.rem(lax.axis_index("space"), 2)

    @pl.loop(0, SLAB)
    def _(p):
        kind = labels[p]
        value = jnp.zeros(kind.shape, jnp.float32)
        for n in range(rates.shape[0]):
            value = jnp.where(kind == n, rates[n], value)
        own[O_KAP + p] = value
        open_cell = 1.0 - electrode[p].astype(jnp.float32)
        own[O_FREE + p] = open_cell
        own[O_INIT + p] = initial[p]
        own[O_MOB + p] = mobility[p]
        for t in range(STEPS):
            own[SLAB * t + p] = 0.5 * source[t, p]
        for out in (far, near):
            out[P_INIT + p] = initial[p]
            out[P_MOB + p] = mobility[p]
            out[P_FREE + p] = open_cell

    for out, begin in ((far, odd), (near, 1 - odd)):

        @pl.loop(0, SLAB - 1)
        def _(j):
            out[P_KAP + j] = own[O_KAP + begin + j]
            for t in range(STEPS):
                out[3 * t + j] = own[SLAB * t + begin + j]


def start_static(odd, fixed, far, near, force, begin, mob, kap, open_cell, done):
    height = fixed.shape[1]
    zero = jnp.zeros((EDGE, mob.shape[2]), jnp.float32)

    @pl.loop(0, mob.shape[0])
    def _(p):
        mob[p, pl.ds(0, EDGE)] = zero
        mob[p, pl.ds(EDGE + height, EDGE)] = zero

    moves = []
    own_at = (O_INIT, O_MOB, O_FREE, O_KAP)
    side_at = (P_INIT, P_MOB, P_FREE, P_KAP)
    for block, count, (i, m, o, k), deep, shallow in (
        (fixed, SLAB, own_at, 4, 3),
        (far, SLAB - 1, side_at, 8 * odd, 7 * odd),
        (near, SLAB - 1, side_at, 8 - 8 * odd, 7 - 7 * odd),
    ):
        window = pl.ds(deep, SLAB)
        moves.append((block.at[pl.ds(m, SLAB)], mob.at[window, pl.ds(EDGE, height)]))
        moves.append((block.at[pl.ds(i, SLAB)], begin.at[window]))
        moves.append((block.at[pl.ds(o, SLAB)], open_cell.at[window]))
        moves.append((block.at[pl.ds(k, count)], kap.at[pl.ds(shallow, count)]))
        for t in range(STEPS):
            moves.append((block.at[pl.ds(count * t, count)], force.at[t, pl.ds(shallow, count)]))
    copies = [pltpu.make_async_copy(here, there, done.at[n]) for n, (here, there) in enumerate(moves)]
    for copy in copies:
        copy.start()
    return copies


def finish(copies):
    for copy in copies:
        copy.wait()


def make_weights(mob, weights, first, last):
    height = mob.shape[1] - 2 * EDGE

    @pl.loop(first, last)
    def _(j):
        for r in range(0, height, 8):
            at = lambda p, d: mob[p, pl.ds(EDGE + r + d, 8)]
            here = at(j + 1, 0)
            lane = lax.broadcasted_iota(jnp.int32, here.shape, 1)
            lowest, highest = lane == 0, lane == here.shape[1] - 1
            xl = 0.5 * (here + at(j, 0))
            xh = 0.5 * (here + at(j + 2, 0))
            yl = 0.5 * (here + at(j + 1, -1))
            yh = 0.5 * (here + at(j + 1, 1))
            zl = 0.5 * (here + jnp.where(lowest, 0.0, shifted(here, 1, 1)))
            zh = 0.5 * (here + jnp.where(highest, 0.0, shifted(here, -1, 1)))
            rows = pl.ds(r, 8)
            weights[j, 0, rows] = xl
            weights[j, 1, rows] = xh
            weights[j, 2, rows] = yl
            weights[j, 3, rows] = yh
            weights[j, 4, rows] = jnp.where(lowest, 0.0, 1.5 * zl)
            weights[j, 5, rows] = jnp.where(highest, 0.0, zh)
            weights[j, 6, rows] = 1.0 + (xl + xh + yl + yh + zl + zh) + 0.5 * zh


def clear_edges(cells):
    zero = jnp.zeros((EDGE, cells.shape[-1]), jnp.float32)

    @pl.loop(0, cells.shape[1])
    def _(p):
        for t in range(STEPS):
            cells[t, p, pl.ds(0, EDGE)] = zero
            cells[t, p, pl.ds(cells.shape[2] - EDGE, EDGE)] = zero


def gathered(w, cells, t, p, r):
    here = cells[t, p, pl.ds(EDGE + r, 8)]
    total = w[0] * cells[t, p - 1, pl.ds(EDGE + r, 8)]
    total += w[1] * cells[t, p + 1, pl.ds(EDGE + r, 8)]
    total += w[2] * cells[t, p, pl.ds(EDGE + r - 1, 8)]
    total += w[3] * cells[t, p, pl.ds(EDGE + r + 1, 8)]
    total += w[4] * shifted(here, 1, 1)
    total += w[5] * shifted(here, -1, 1)
    return here, total


def run_sweep(cells, other, weights, kap, open_cell, force, opening, done=0):
    height = cells.shape[2] - 2 * EDGE
    for number in range(done, PASSES):
        source, target = (cells, other) if number % 2 == 0 else (other, cells)

        @pl.loop(number, 10 - number)
        def _(j):
            for r in range(0, height, 8):
                rows = pl.ds(r, 8)
                w = [weights[j, n, rows] for n in range(7)]
                rate = kap[j, rows]
                gain = DAMPING * open_cell[j + 1, rows]
                former = opening[j, rows]
                for t in range(STEPS):
                    here, total = gathered(w, source, t, j + 1, r)
                    pull = rate * jnp.abs(here)
                    residue = force[t, j, rows] + former + total - here * (w[6] + 0.5 * pull)
                    target[t, j + 1, pl.ds(EDGE + r, 8)] = here + gain * residue / (w[6] + pull)
                    former = here


def first_pass(cells, other, weights, kap, open_cell, force):
    height = cells.shape[2] - 2 * EDGE

    @pl.loop(0, 10)
    def _(j):
        for r in range(0, height, 8):
            rows = pl.ds(r, 8)
            w = [weights[j, n, rows] for n in range(7)]
            here, total = gathered(w, cells, 0, j + 1, r)
            pull = kap[j, rows] * jnp.abs(here)
            shared = here + total - here * (w[6] + 0.5 * pull)
            gain = DAMPING * open_cell[j + 1, rows] / (w[6] + pull)
            for t in range(STEPS):
                other[t, j + 1, pl.ds(EDGE + r, 8)] = here + gain * (force[t, j, rows] + shared)


def halved(read):
    return 0.25 * ((read(0, 0) + read(0, 1)) + (read(1, 0) + read(1, 1)))


def first_kernel(who, fixed, far, near, to_far, to_near, closing,
                 force, begin, mob, kap, open_cell, weights, cells, other, rough, done):
    odd = who[0]
    height = fixed.shape[1]
    copies = start_static(odd, fixed, far, near, force, begin, mob, kap, open_cell, done)
    clear_edges(cells)
    clear_edges(other)
    finish(copies)
    make_weights(mob, weights, 0, 10)

    @pl.loop(0, 12)
    def _(p):
        cells[0, p, pl.ds(EDGE, height)] = begin[p]

    first_pass(cells, other, weights, kap, open_cell, force)
    run_sweep(cells, other, weights, kap, open_cell, force, begin.at[pl.ds(1, 10)], 1)
    for p in range(SLAB):
        closing[p] = cells[STEPS - 1, 4 + p, pl.ds(EDGE, height)]
    half = height // 2
    for a in range(6):
        rough[a] = halved(lambda x, y: mob[2 * a + x, pl.ds(EDGE + y, half, stride=2)])
    for out, base in ((to_far, 4 - 4 * odd), (to_near, 4 * odd)):
        for t in range(STEPS):
            for p in range(SLAB):
                out[4 * t + p] = cells[t, 4 + p, pl.ds(EDGE, height)]
        out[16, pl.ds(0, half)] = rough[base]
        out[16, pl.ds(half, half)] = rough[base + 1]


def residual_kernel(who, fixed, far, near, own, low_far, low_near, arriving,
                    base, closing, both, rhs, rough, force, begin, mob, kap, open_cell, weights, cells, residues, done):
    odd, leading, place, count = who[0], who[1], who[2], who[3]
    height = fixed.shape[1]
    half = height // 2
    copies = start_static(odd, fixed, far, near, force, begin, mob, kap, open_cell, done)
    clear_edges(cells)
    rows = pl.ds(EDGE, height)
    for t in range(STEPS):

        @pl.loop(0, SLAB)
        def _(p):
            cells[t, 4 + p, rows] = own[4 * t + p]
            cells[t, 8 * odd + p, rows] = low_far[4 * t + p]
            cells[t, 8 - 8 * odd + p, rows] = low_near[4 * t + p]

    finish(copies)
    make_weights(mob, weights, 1, 9)

    @pl.loop(1, 9)
    def _(j):
        for r in range(0, height, 8):
            rows = pl.ds(r, 8)
            w = [weights[j, n, rows] for n in range(7)]
            rate = kap[j, rows]
            former = jnp.where(leading == 1, begin[j + 1, rows], 0.0)
            acc = jnp.zeros_like(former)
            for t in range(STEPS):
                here, total = gathered(w, cells, t, j + 1, r)
                pull = rate * jnp.abs(here)
                acc += force[t, j, rows] + former + total - here * (w[6] + 0.5 * pull)
                former = here
            residues[j - 1, rows] = acc

    for a in range(4):
        coarse = 2 * place - 1 + a
        inside = jnp.logical_and(coarse >= 0, coarse < 2 * count)
        value = halved(lambda x, y: residues[2 * a + x, pl.ds(y, half, stride=2)])
        base[a] = jnp.where(inside, value, 0.0)
        closing[a] = halved(lambda x, y: cells[STEPS - 1, 2 + 2 * a + x, pl.ds(EDGE + y, half, stride=2)])
        both[0, a] = base[a]
        both[1, a] = closing[a]
    for a in range(2):
        rhs[a] = base[1 + a] + halved(lambda x, y: arriving[2 * a + x, pl.ds(y, half, stride=2)])
        for block, at in ((low_far, 8 * odd), (low_near, 8 - 8 * odd)):
            rough[at + a] = block[16, pl.ds(half * a, half)]
    for a in range(6):
        rough[2 + a] = halved(lambda x, y: mob[2 * a + x, pl.ds(EDGE + y, half, stride=2)])


def join_kernel(who, side_far, side_near, pair, rough, arriving, pairs, roughs, opening):
    odd = who[0]
    half = pair.shape[2]
    for a in range(2):
        for q in range(2):
            pairs[q, 2 + a] = pair[q, a]
    for a in range(10):
        roughs[2 + a] = rough[a]
    for p in range(SLAB):
        opening[3 + p] = arriving[p]
    for block, up in ((side_far, odd), (side_near, 1 - odd)):
        for a in range(2):
            rows = pl.ds(half * a, half)
            for q in range(2):
                pairs[q, 4 * up + a] = block[q, rows]
            roughs[12 * up + a] = block[2, rows]
        for j in range(SLAB - 1):
            opening[7 * up + j] = block[3 + j]


def last_kernel(who, fixed, far, near, own, low_far, low_near, arriving, correction,
                out, force, begin, mob, kap, open_cell, weights, cells, other, opening, done):
    odd, leading = who[0], who[1]
    height = fixed.shape[1]
    half = height // 2
    copies = start_static(odd, fixed, far, near, force, begin, mob, kap, open_cell, done)
    clear_edges(cells)
    clear_edges(other)
    finish(copies)
    make_weights(mob, weights, 0, 10)
    for y in range(2):
        rows = pl.ds(y, half, stride=2)
        into = pl.ds(EDGE + y, half, stride=2)

        @pl.loop(0, SLAB)
        def _(p):
            for block, at in ((own, 4), (low_far, 8 * odd), (low_near, 8 - 8 * odd)):
                plane = at + p
                change = open_cell[plane, rows] * correction[0, plane // 2]
                for t in range(STEPS):
                    cells[t, plane, into] = block[4 * t + p, rows] + change

        @pl.loop(0, 10)
        def _(j):
            base = jnp.where(leading == 1, begin[j + 1, rows], arriving[j, rows])
            opening[j, rows] = base + open_cell[j + 1, rows] * correction[1, (j + 1) // 2]

    run_sweep(cells, other, weights, kap, open_cell, force, opening)
    for t in range(STEPS):
        for p in range(SLAB):
            out[t, p] = cells[t, 4 + p, pl.ds(EDGE, height)]


def windows(height, depth):
    plane = (height, depth)
    tall = (height + 2 * EDGE, depth)
    f32 = jnp.float32
    return [
        pltpu.VMEM((STEPS, 10) + plane, f32),
        pltpu.VMEM((12,) + plane, f32),
        pltpu.VMEM((12,) + tall, f32),
        pltpu.VMEM((10,) + plane, f32),
        pltpu.VMEM((12,) + plane, f32),
        pltpu.VMEM((10, 7) + plane, f32),
    ]


def call(kernel, name, inputs, outputs, scratch, grant=24, held=3):
    return pl.pallas_call(
        kernel,
        out_shape=[jax.ShapeDtypeStruct(o, jnp.float32) for o in outputs],
        in_specs=[SMEM] + [HBM, ANY, ANY][:held] + [VMEM] * (len(inputs) - 1 - held),
        out_specs=[VMEM] * len(outputs),
        scratch_shapes=scratch + [pltpu.SemaphoreType.DMA((24,))] * (held > 0),
        name=name,
        compiler_params=pltpu.CompilerParams(vmem_limit_bytes=grant << 20),
    )(*inputs)


def inner(values, dim, cut):
    return lax.slice_in_dim(values, cut, values.shape[dim] - cut, axis=dim)


class Coupling:
    def __init__(self, mob, inside):
        centre = mob[1:-1]
        padded = jnp.pad(centre, ((0, 0), (1, 1), (1, 1)))
        keep = inside[1:-1, None, None]
        half = 0.5 * LATERAL * keep
        axial = 0.5 * AXIAL * keep
        self.xl = half * (centre + mob[:-2])
        self.xh = half * (centre + mob[2:])
        self.yl = half * (centre + padded[:, :-2, 1:-1])
        self.yh = half * (centre + padded[:, 2:, 1:-1])
        self.zl = axial * (centre + padded[:, 1:-1, :-2])
        self.zh = axial * (centre + padded[:, 1:-1, 2:])
        self.own = keep - (self.xl + self.xh + self.yl + self.yh + self.zl + self.zh)

    def step(self, values):
        planes = values.shape[-3] - 2
        cut = (self.own.shape[0] - planes) // 2
        take = lambda w: inner(w, 0, cut)
        centre = values[..., 1:-1, :, :]
        pads = [(0, 0)] * (values.ndim - 2) + [(1, 1), (1, 1)]
        padded = jnp.pad(centre, pads)
        return (
            take(self.own) * centre
            + take(self.xl) * values[..., :-2, :, :]
            + take(self.xh) * values[..., 2:, :, :]
            + take(self.yl) * padded[..., :-2, 1:-1]
            + take(self.yh) * padded[..., 2:, 1:-1]
            + take(self.zl) * padded[..., 1:-1, :-2]
            + take(self.zh) * padded[..., 1:-1, 2:]
        )

    def steps(self, values, count):
        for number in range(count):
            values = self.step(values)
        return values


def sent(value, steps, to):
    times = lax.axis_size("tm")
    count = lax.axis_size("space")
    pairs = [
        (k * count + i, (k + steps) * count + to[i])
        for k in range(times - steps)
        for i in range(count)
        if 0 <= to[i] < count
    ]
    return lax.ppermute(value, ("tm", "space"), pairs)


def traded(far, near):
    count = lax.axis_size("space")
    far_of = [i + 1 if i % 2 else i - 1 for i in range(count)]
    return sent(far, 0, far_of), sent(near, 0, [i ^ 1 for i in range(count)])


def by_side(odd, far, near):
    return jnp.where(odd, near, far), jnp.where(odd, far, near)


def arrived(value, steps):
    times = lax.axis_size("tm")
    return lax.ppermute(value, "tm", [(k, k + steps) for k in range(times - steps)])


def on_device(source, initial, mobility, labels, electrode, rates):
    _, height, depth = initial.shape
    plane = (height, depth)
    place = lax.axis_index("space")
    odd = place % 2
    leading = lax.axis_index("tm") == 0
    who = jnp.stack([odd, leading.astype(jnp.int32), place, jnp.int32(lax.axis_size("space"))]).astype(jnp.int32)
    inside = lambda reach: (
        (2 * place + jnp.arange(-reach, 2 + reach) >= 0)
        & (2 * place + jnp.arange(-reach, 2 + reach) < 2 * lax.axis_size("space"))
    ).astype(jnp.float32)

    fields = (source, initial, mobility, labels, electrode)
    far, near, fixed = pl.pallas_call(
        parcel_kernel,
        out_shape=[jax.ShapeDtypeStruct((n,) + plane, jnp.float32) for n in (PARCEL, PARCEL, OWN)],
        in_specs=[SMEM] + [VMEM] * len(fields),
        out_specs=[VMEM] * 3,
        name="parcel",
        compiler_params=pltpu.CompilerParams(vmem_limit_bytes=60 << 20),
    )(rates, *fields)
    far, near = traded(far, near)
    fixed = pltpu.with_memory_space_constraint(fixed, pltpu.HBM)
    static = (who, fixed, far, near)
    tall = (height + 2 * EDGE, depth)

    coarse = (height // 2, depth)
    to_far, to_near, closing = call(
        first_kernel,
        "first",
        static,
        [(17,) + plane] * 2 + [initial.shape],
        windows(height, depth) + [pltpu.VMEM((STEPS, 12) + tall, jnp.float32)] * 2
        + [pltpu.VMEM((6,) + coarse, jnp.float32)],
    )
    got_far, got_near = traded(to_far, to_near)
    opening = arrived(closing, 1)
    states = (to_far, got_far, got_near)

    base, closing, both, rhs, rough_w = call(
        residual_kernel,
        "residual",
        static + states + (opening,),
        [(4,) + coarse] * 2 + [(2, 4) + coarse, (2,) + coarse, (10,) + coarse],
        windows(height, depth)
        + [pltpu.VMEM((STEPS, 12) + tall, jnp.float32), pltpu.VMEM((8,) + plane, jnp.float32)],
    )
    one = arrived(base, 1)
    two = arrived(both, 2)
    three = arrived(closing, 3)
    rhs1 = one + two[1]
    rhs2 = two[0] + three
    pair = jnp.stack([rhs, inner(rhs1, 0, 1)])
    pair = pair + Coupling(inner(rough_w, 0, 3), inside(1)).step(jnp.stack([rhs1, rhs2]))

    flat = lambda v: v.reshape((-1,) + plane)
    cargo = lambda c, o: jnp.concatenate([flat(pair), flat(c), o], axis=0)
    to_low = cargo(rough_w[8:10], opening[: SLAB - 1])
    to_high = cargo(rough_w[0:2], opening[1:])
    side_far, side_near = traded(*by_side(odd == 1, to_low, to_high))
    pair, rough_far, opening = call(
        join_kernel,
        "join",
        (who, side_far, side_near, pair, rough_w, opening),
        [(2, 6) + coarse, (14,) + coarse, (10,) + plane],
        [],
        12,
        0,
    )
    joined = lambda *parts: jnp.concatenate(parts, axis=1)
    count = lax.axis_size("space")
    gap = jnp.zeros_like(pair[:, :2])
    got = sent(pair, 2, [i if i in (0, count - 1) else i + 1 if i % 2 else i - 1 for i in range(count)])
    got = jnp.where(place == 0, joined(gap, got[:, :4]), got)
    got = jnp.where(place == count - 1, joined(got[:, 2:], gap), got)
    mate = sent(got, 0, [i ^ 1 for i in range(count)])
    older = jnp.where(odd == 1, joined(mate[:, 2:], got), joined(got, mate[:, :4]))
    coupling = Coupling(rough_far, inside(6))
    pair = pair + coupling.steps(older, 2)
    got = joined(sent(pair, 4, [i - 2 if i % 2 else i + 2 for i in range(count)]), sent(pair[:, 2:4], 4, range(count)))
    mate = sent(got, 0, [i ^ 1 for i in range(count)])
    centre, beside = got[:, 6:], mate[:, 6:]
    older = jnp.where(
        odd == 1,
        joined(mate[:, 2:6], beside, centre, got[:, :6]),
        joined(got[:, :6], centre, beside, mate[:, :4]),
    )
    correction = pair + coupling.steps(older, 4)

    (density,) = call(
        last_kernel,
        "last",
        static + states + (opening, correction),
        [source.shape],
        windows(height, depth)
        + [pltpu.VMEM((STEPS, 12) + tall, jnp.float32)] * 2
        + [pltpu.VMEM((10,) + plane, jnp.float32)],
    )
    return density


def solution(mesh):
    cells = P("space", None, None)
    times = P("tm", "space", None, None)
    return jax.shard_map(
        on_device,
        mesh=mesh,
        in_specs=(times, cells, cells, cells, cells, P()),
        out_specs=times,
        check_vma=False,
    )
```
